768 devices in a mesh: energy: 32 (over y, z_hi), col: 24 (over z_lo, x, core).
Axes of the slice: x: 4, y: 8, z: 12 (z_hi: 4, z_lo: 3; z = z_hi * 3 + z_lo), core: 2. Of those that a mesh axis runs over, the one named last changes fastest.
Arguments:
- lesser: float32 [512, 2, 72, 1152], P('energy', None, 'col'), may hold values from -6 to 6
- greater_transposed: float32 [512, 2, 72, 1152], P('energy', None, 'col'), may hold values from -6 to 6
- coulomb: bfloat16 [1152, 1152], P('energy', 'col'), may hold values from -0.1875 to 0.1875
Outputs:
- screened: float32 [512, 2, 72, 1152], P('energy', None, 'col')
The draws below stay inside these ranges and needn't reach their ends.
All inputs are finite; a program needn't handle non-finite values.
Results may differ from the reference program's by a relative error of at most 0.0029.
Values may be sent and summed in bfloat16 or wider, within the bound.
No kernel may reach another device: no remote copies, remote signals or barrier semaphores. Data moves between devices by JAX's collectives and lax.ppermute only.
A program may use at most 64 MiB of HBM per device.

```python
import math
import jax
import jax.numpy as jnp

NB = 1152
ENERGIES = 512
COLS = 72


def block_levels(own_key, extent, split, low, high):
    def one(position, shards_of):
        steps = jax.random.uniform(jax.random.fold_in(jax.random.fold_in(own_key, 6), position), (shards_of,), jnp.float32, low / len(split), high / len(split))
        return jnp.repeat(jnp.exp(steps), extent[position] // shards_of).reshape((-1,) + (1,) * (len(extent) - position - 1))

    gain = one(*split[0])
    for cut in split[1:]:
        gain = gain * one(*cut)
    return gain


def noise(stream_key, extent, width, limit, pieces=(), dtype=jnp.bfloat16):
    gain = block_levels(stream_key, extent, pieces, -0.22, 0.18) if pieces else 1.0
    result = jax.random.normal(stream_key, extent, jnp.float32) * width * gain
    return jnp.minimum(jnp.maximum(result, -limit), limit).astype(dtype)


def setup_inputs(seed: int = 0) -> dict:
    keys = jax.random.split(jax.random.key(seed), 4)
    lesser = noise(keys[0], (ENERGIES, 2, COLS, NB), 1.0, 6.0, ((0, 32), (2, 24)), jnp.float32)
    greater_transposed = noise(keys[1], (ENERGIES, 2, COLS, NB), 1.0, 6.0, ((0, 32), (2, 24)), jnp.float32)
    coulomb = noise(keys[2], (NB, NB), NB ** -0.5, 0.1875, ((0, 32), (1, 24)))
    return {"lesser": lesser, "greater_transposed": greater_transposed, "coulomb": coulomb}


def reference(lesser, greater_transposed, coulomb):
    energies = lesser.shape[0]
    padded = 2 * energies
    left = lesser[:, 0] + 1j * lesser[:, 1]
    right = greater_transposed[:, 0] + 1j * greater_transposed[:, 1]
    left_hat = jnp.fft.fft(left, n=padded, axis=0)
    right_pad = jnp.pad(right, ((0, energies), (0, 0), (0, 0)))
    right_flip = jnp.roll(jnp.flip(right_pad, 0), 1, axis=0)
    corr = jnp.fft.ifft(left_hat * jnp.fft.fft(right_flip, axis=0), axis=0)[:energies]
    factor = 1.0 / math.sqrt(energies)
    polarized = jnp.stack([corr.imag * factor, -corr.real * factor], axis=1).astype(jnp.bfloat16)
    flattened = polarized.reshape(-1, coulomb.shape[0])
    screened = jnp.dot(flattened, coulomb, preferred_element_type=jnp.float32)
    return screened.reshape(lesser.shape)
```

```python
import functools
import math

import jax
import jax.numpy as jnp
import numpy as np
from jax import lax
from jax.experimental import pallas as pl
from jax.experimental.layout import Layout, with_layout_constraint
from jax.experimental.pallas import tpu as pltpu
from jax.sharding import PartitionSpec as P

LANES = 128
RADIX = 8
HALF = math.sqrt(0.5)
SCALE = 4096.0


def split(x):
    high = x.astype(jnp.bfloat16)
    return high, (x - high.astype(jnp.float32)).astype(jnp.bfloat16)


def turn(re, im, eighths):
    eighths %= 8
    if eighths % 2:
        re, im = (re + im) * HALF, (im - re) * HALF
        eighths -= 1
    return ((re, im), (im, -re), (-re, -im), (-im, re))[eighths // 2]


def pack_kernel(lesser_ref, greater_ref, out_ref):
    energies = out_ref.shape[3]
    stride = lesser_ref.shape[0] // energies
    blocks = stride // 2
    for which, ref in enumerate((lesser_ref, greater_ref)):
        for block in range(blocks):
            for part in range(2):
                out_ref[block, which, part] = ref[pl.ds(block * 2 + part, energies, stride=stride), :]
    out_ref[blocks:] = jnp.zeros_like(out_ref[blocks:])


def correlate_kernel(x_ref, high_ref, low_ref, twiddle_ref, out_ref, total_ref, spread_ref):
    sources, here, lanes = x_ref.shape[0], x_ref.shape[1] // 4, x_ref.shape[2]
    points = high_ref.shape[0] // 2
    pieces = sources * here // points
    per_piece = sources // pieces
    high, low = high_ref[...], low_ref[...]

    def dft(re, im):
        x = jnp.concatenate([re, im], axis=0)
        x_high, x_low = split(x)
        y = jnp.dot(high, x_high, preferred_element_type=jnp.float32)
        y += jnp.dot(high, x_low, preferred_element_type=jnp.float32)
        return y + jnp.dot(low, x_high, preferred_element_type=jnp.float32)

    def piece(which, part, j):
        at = (which * 2 + part) * here
        return x_ref[j * per_piece:(j + 1) * per_piece, at:at + here, :].reshape(points, lanes)

    for r in range(RADIX // 2):
        for other in (r, r + RADIX // 2):
            spread_ref[2 * other] = jnp.broadcast_to(twiddle_ref[:, 2 * other:2 * other + 1], (points, lanes))
            spread_ref[2 * other + 1] = jnp.broadcast_to(twiddle_ref[:, 2 * other + 1:2 * other + 2], (points, lanes))
        sums = []
        for which in range(2):
            terms = []
            for j in range(4):
                re, im = piece(which, 0, j), piece(which, 1, j)
                if which:
                    im = -im
                terms.append(turn(re, im, r * j))
            even = [terms[0][k] + terms[2][k] for k in range(2)]
            odd = [terms[1][k] + terms[3][k] for k in range(2)]
            sums.append(([even[k] + odd[k] for k in range(2)], [even[k] - odd[k] for k in range(2)]))
        mixed = []
        for half, other in enumerate((r, r + RADIX // 2)):
            w_re, w_im = spread_ref[2 * other], spread_ref[2 * other + 1]
            turned = []
            for which in range(2):
                re, im = sums[which][half]
                turned.append((re * w_re - im * w_im, re * w_im + im * w_re))
            y = dft(
                jnp.concatenate([turned[0][0], turned[1][0]], axis=1),
                jnp.concatenate([turned[0][1], turned[1][1]], axis=1),
            )
            l_re, l_im = y[:points, :lanes], y[points:, :lanes]
            g_re, g_im = y[:points, lanes:], y[points:, lanes:]
            mixed.append((l_re * g_re + l_im * g_im, l_re * g_im - l_im * g_re))
        z = dft(
            jnp.concatenate([mixed[0][0], mixed[1][0]], axis=1),
            jnp.concatenate([mixed[0][1], mixed[1][1]], axis=1),
        )
        back = []
        for half, other in enumerate((r, r + RADIX // 2)):
            w_re, w_im = spread_ref[2 * other], spread_ref[2 * other + 1]
            re, im = z[:points, half * lanes:(half + 1) * lanes], z[points:, half * lanes:(half + 1) * lanes]
            back.append((re * w_re - im * w_im, re * w_im + im * w_re))
        both = [back[0][k] + back[1][k] for k in range(2)]
        apart = [back[0][k] - back[1][k] for k in range(2)]
        for j in range(4):
            re, im = turn(*(apart if j % 2 else both), r * j)
            if r == 0:
                total_ref[j, 0] = re
                total_ref[j, 1] = im
            else:
                total_ref[j, 0] += re
                total_ref[j, 1] += im
    energies = sources * here
    factor = -1.0 / (math.sqrt(energies) * 2 * energies * SCALE * SCALE)
    for j in range(pieces):
        for part in range(2):
            value = (total_ref[j, 1 - part] * factor).astype(jnp.bfloat16)
            out_ref[j * per_piece:(j + 1) * per_piece, part * here:(part + 1) * here, :] = value.reshape(
                per_piece, here, lanes
            )


def screen_kernel(polar_ref, coulomb_ref, out_ref):
    order = coulomb_ref.shape[0]
    groups = order // LANES
    here = polar_ref.shape[1] // 2
    stride = out_ref.shape[0] // here
    columns = stride // 2 // groups
    rows = [
        jnp.concatenate([polar_ref[c * groups + k] for k in range(groups)], axis=1) for c in range(columns)
    ]
    product = lax.dot_general(
        jnp.concatenate(rows, axis=0), coulomb_ref[...], (((1,), (1,)), ((), ())), preferred_element_type=jnp.float32
    )
    for c in range(columns):
        for part in range(2):
            at = (c * 2 + part) * here
            for k in range(groups):
                out_ref[pl.ds((c * groups + k) * 2 + part, here, stride=stride), :] = product[
                    at:at + here, k * LANES:(k + 1) * LANES
                ]


def tables(energies):
    points = energies * 2 // RADIX
    angle = np.outer(np.arange(points), np.arange(points)) % points * (2 * np.pi / points)
    cos, sin = np.cos(angle), np.sin(angle)
    whole = np.block([[cos, sin], [-sin, cos]])
    high = whole.astype(jnp.bfloat16)
    low = (whole - high.astype(np.float64)).astype(jnp.bfloat16)
    twiddle = np.zeros((points, LANES), np.float32)
    for r in range(RADIX):
        turned = np.arange(points) * r * (np.pi / energies)
        twiddle[:, 2 * r], twiddle[:, 2 * r + 1] = np.cos(turned), -np.sin(turned)
    return high, low, twiddle


def rows_view(x):
    energies, _, columns, order = x.shape
    x = x.reshape(energies, 2, columns, order // LANES, LANES).transpose(0, 2, 3, 1, 4)
    x = with_layout_constraint(x, Layout(tuple(range(x.ndim))))
    return x.reshape(-1, LANES)


def pack(lesser, greater, owners):
    here = lesser.shape[0]
    return pl.pallas_call(
        pack_kernel,
        out_shape=jax.ShapeDtypeStruct((owners, 2, 2, here, LANES), jnp.float32),
        compiler_params=pltpu.CompilerParams(vmem_limit_bytes=16 << 20),
        name="pack",
    )(rows_view(lesser), rows_view(greater))


def correlate(x):
    owners, _, _, here, lanes = x.shape
    energies = owners * here
    points = energies * 2 // RADIX
    high, low, twiddle = tables(energies)
    return pl.pallas_call(
        correlate_kernel,
        out_shape=jax.ShapeDtypeStruct((owners, 2 * here, lanes), jnp.bfloat16),
        scratch_shapes=[
            pltpu.VMEM((4, 2, points, lanes), jnp.float32),
            pltpu.VMEM((2 * RADIX, points, lanes), jnp.float32),
        ],
        compiler_params=pltpu.CompilerParams(vmem_limit_bytes=24 << 20),
        name="correlate",
    )(x.reshape(owners, 4 * here, lanes), jnp.asarray(high), jnp.asarray(low), jnp.asarray(twiddle))


def screen(polar, coulomb, shape):
    energies, _, columns, order = shape
    out = pl.pallas_call(
        screen_kernel,
        out_shape=jax.ShapeDtypeStruct((energies * columns * order * 2 // LANES, LANES), jnp.float32),
        compiler_params=pltpu.CompilerParams(vmem_limit_bytes=24 << 20),
        name="screen",
    )(polar, coulomb)
    out = out.reshape(energies, columns, order // LANES, 2, LANES).transpose(0, 1, 3, 2, 4)
    return out.reshape(energies, columns, 2, order).transpose(0, 2, 1, 3)


def per_device(lesser, greater_transposed, coulomb):
    owners = lax.axis_size("energy")
    packed = pack(lesser, greater_transposed, owners)
    sent = (packed * SCALE).astype(jnp.float16)
    got = lax.all_to_all(sent, "energy", split_axis=0, concat_axis=0, tiled=True)
    polar = correlate(got.astype(jnp.float32))
    polar = lax.all_to_all(polar, "energy", split_axis=0, concat_axis=0, tiled=True)
    mine = lax.all_gather(coulomb.T, "energy", axis=1, tiled=True)
    coulomb_t = lax.all_gather(mine, "col", axis=0, tiled=True)
    return screen(polar, coulomb_t, lesser.shape)


def solution(mesh):
    placed = (P("energy", None, "col", None), P("energy", None, "col", None), P("energy", "col"))
    return jax.shard_map(
        per_device,
        mesh=mesh,
        in_specs=placed,
        out_specs=P("energy", None, "col", None),
        check_vma=False,
    )
```

```python
import functools
import math

import jax
import jax.numpy as jnp
import numpy as np
from jax import lax
from jax.experimental import pallas as pl
from jax.experimental.layout import Layout, with_layout_constraint
from jax.experimental.pallas import tpu as pltpu
from jax.sharding import PartitionSpec as P

LANES = 128
RADIX = 8
RUN, ACROSS, CORES = 3, 4, 2
HALF = math.sqrt(0.5)
COULOMB_SCALE = float(2**18)
SCALE = 4096.0


def split(x):
    high = x.astype(jnp.bfloat16)
    return high, (x - high.astype(jnp.float32)).astype(jnp.bfloat16)


def turn(re, im, eighths):
    eighths %= 8
    if eighths % 2:
        re, im = (re + im) * HALF, (im - re) * HALF
        eighths -= 1
    return ((re, im), (im, -re), (-re, -im), (-im, re))[eighths // 2]


def pack_kernel(lesser_ref, greater_ref, coulomb_ref, place_ref, out_ref):
    extra = out_ref.shape[1] // 5
    here = extra
    stride = lesser_ref.shape[0] // here
    blocks = stride // 2
    for which, ref in enumerate((lesser_ref, greater_ref)):
        for block in range(blocks):
            for part in range(2):
                at = (which * 2 + part) * here
                out_ref[block, at:at + here, :] = ref[pl.ds(block * 2 + part, here, stride=stride), :] * SCALE
    out_ref[blocks:, :4 * here, :] = jnp.zeros_like(out_ref[blocks:, :4 * here, :])
    block = coulomb_ref[...]
    total = None
    for group in range(block.shape[1] // extra):
        turned = lax.dot_general(
            block, place_ref[group], (((0,), (0,)), ((), ())), preferred_element_type=jnp.float32
        )[group * extra:(group + 1) * extra, :]
        total = turned if total is None else total + turned
    total = total * COULOMB_SCALE
    for owner in range(out_ref.shape[0]):
        out_ref[owner, 4 * here:, :] = total


def unpack_kernel(x_ref, out_ref):
    sources, rows, _ = x_ref.shape
    extra = rows // 5
    width = out_ref.shape[1] // sources
    for group in range(out_ref.shape[0] // extra):
        pieces = [
            x_ref[source, 4 * extra:, group * width:(group + 1) * width] for source in range(sources)
        ]
        row = jnp.concatenate(pieces, axis=1) * (1.0 / COULOMB_SCALE)
        out_ref[group * extra:(group + 1) * extra, :] = row.astype(jnp.bfloat16)


def correlate_kernel(x_ref, high_ref, low_ref, twiddle_ref, out_ref, total_ref, spread_ref):
    sources, here, lanes = x_ref.shape[0], x_ref.shape[1] // 5, x_ref.shape[2]
    points = high_ref.shape[0] // 2
    pieces = sources * here // points
    per_piece = sources // pieces
    high, low = high_ref[...], low_ref[...]

    def dft(re, im):
        x = jnp.concatenate([re, im], axis=0)
        x_high, x_low = split(x)
        y = jnp.dot(high, x_high, preferred_element_type=jnp.float32)
        y += jnp.dot(high, x_low, preferred_element_type=jnp.float32)
        return y + jnp.dot(low, x_high, preferred_element_type=jnp.float32)

    def piece(which, part, j):
        at = (which * 2 + part) * here
        return x_ref[j * per_piece:(j + 1) * per_piece, at:at + here, :].reshape(points, lanes)

    for r in range(RADIX // 2):
        for other in (r, r + RADIX // 2):
            spread_ref[2 * other] = jnp.broadcast_to(twiddle_ref[:, 2 * other:2 * other + 1], (points, lanes))
            spread_ref[2 * other + 1] = jnp.broadcast_to(twiddle_ref[:, 2 * other + 1:2 * other + 2], (points, lanes))
        sums = []
        for which in range(2):
            terms = []
            for j in range(4):
                re, im = piece(which, 0, j), piece(which, 1, j)
                if which:
                    im = -im
                terms.append(turn(re, im, r * j))
            even = [terms[0][k] + terms[2][k] for k in range(2)]
            odd = [terms[1][k] + terms[3][k] for k in range(2)]
            sums.append(([even[k] + odd[k] for k in range(2)], [even[k] - odd[k] for k in range(2)]))
        mixed = []
        for half, other in enumerate((r, r + RADIX // 2)):
            w_re, w_im = spread_ref[2 * other], spread_ref[2 * other + 1]
            turned = []
            for which in range(2):
                re, im = sums[which][half]
                turned.append((re * w_re - im * w_im, re * w_im + im * w_re))
            y = dft(
                jnp.concatenate([turned[0][0], turned[1][0]], axis=1),
                jnp.concatenate([turned[0][1], turned[1][1]], axis=1),
            )
            l_re, l_im = y[:points, :lanes], y[points:, :lanes]
            g_re, g_im = y[:points, lanes:], y[points:, lanes:]
            mixed.append((l_re * g_re + l_im * g_im, l_re * g_im - l_im * g_re))
        z = dft(
            jnp.concatenate([mixed[0][0], mixed[1][0]], axis=1),
            jnp.concatenate([mixed[0][1], mixed[1][1]], axis=1),
        )
        back = []
        for half, other in enumerate((r, r + RADIX // 2)):
            w_re, w_im = spread_ref[2 * other], spread_ref[2 * other + 1]
            re, im = z[:points, half * lanes:(half + 1) * lanes], z[points:, half * lanes:(half + 1) * lanes]
            back.append((re * w_re - im * w_im, re * w_im + im * w_re))
        both = [back[0][k] + back[1][k] for k in range(2)]
        apart = [back[0][k] - back[1][k] for k in range(2)]
        for j in range(4):
            re, im = turn(*(apart if j % 2 else both), r * j)
            if r == 0:
                total_ref[j, 0] = re
                total_ref[j, 1] = im
            else:
                total_ref[j, 0] += re
                total_ref[j, 1] += im
    energies = sources * here
    factor = -1.0 / (math.sqrt(energies) * 2 * energies * SCALE * SCALE)
    for j in range(pieces):
        for part in range(2):
            value = (total_ref[j, 1 - part] * factor).astype(jnp.bfloat16)
            out_ref[j * per_piece:(j + 1) * per_piece, part * here:(part + 1) * here, :] = value.reshape(
                per_piece, here, lanes
            )


def piece_hops():
    return [(z, x, core) for core in range(CORES) for x in range(ACROSS) for z in range(RUN)]


def source_of(at, hops):
    z, x, core = lax.div(at, ACROSS * CORES), lax.rem(lax.div(at, CORES), ACROSS), lax.rem(at, CORES)
    z, x, core = lax.rem(z + hops[0], RUN), lax.rem(x + hops[1], ACROSS), lax.rem(core + hops[2], CORES)
    return (z * ACROSS + x) * CORES + core


def screen_kernel(index_ref, polar_ref, *refs):
    *pieces, out_ref, coulomb_ref = refs
    wide, order = pieces[0].shape
    groups = order // LANES
    here = polar_ref.shape[1] // 2
    stride = out_ref.shape[0] // here
    columns = stride // 2 // groups
    me = index_ref[0]
    for hops, piece in zip(piece_hops(), pieces):
        coulomb_ref[source_of(me, hops)] = piece[...]
    rows = [
        jnp.concatenate([polar_ref[c * groups + k] for k in range(groups)], axis=1) for c in range(columns)
    ]
    product = lax.dot_general(
        jnp.concatenate(rows, axis=0),
        coulomb_ref[...].reshape(order, order),
        (((1,), (1,)), ((), ())),
        preferred_element_type=jnp.float32,
    )
    for c in range(columns):
        for part in range(2):
            at = (c * 2 + part) * here
            for k in range(groups):
                out_ref[pl.ds((c * groups + k) * 2 + part, here, stride=stride), :] = product[
                    at:at + here, k * LANES:(k + 1) * LANES
                ]


def tables(energies):
    points = energies * 2 // RADIX
    angle = np.outer(np.arange(points), np.arange(points)) % points * (2 * np.pi / points)
    cos, sin = np.cos(angle), np.sin(angle)
    whole = np.block([[cos, sin], [-sin, cos]])
    high = whole.astype(jnp.bfloat16)
    low = (whole - high.astype(np.float64)).astype(jnp.bfloat16)
    twiddle = np.zeros((points, LANES), np.float32)
    for r in range(RADIX):
        turned = np.arange(points) * r * (np.pi / energies)
        twiddle[:, 2 * r], twiddle[:, 2 * r + 1] = np.cos(turned), -np.sin(turned)
    return high, low, twiddle


def rows_view(x):
    energies, _, columns, order = x.shape
    x = x.reshape(energies, 2, columns, order // LANES, LANES).transpose(0, 2, 3, 1, 4)
    x = with_layout_constraint(x, Layout(tuple(range(x.ndim))))
    return x.reshape(-1, LANES)


def pack(lesser, greater, coulomb, owners):
    here = lesser.shape[0]
    rows, wide = coulomb.shape
    groups = wide // here
    place = np.zeros((groups, rows, LANES), np.float32)
    for group in range(groups):
        place[group, np.arange(rows), group * rows + np.arange(rows)] = 1
    return pl.pallas_call(
        pack_kernel,
        out_shape=jax.ShapeDtypeStruct((owners, 5 * here, LANES), jnp.float32),
        compiler_params=pltpu.CompilerParams(vmem_limit_bytes=16 << 20),
        name="pack",
    )(rows_view(lesser), rows_view(greater), coulomb, jnp.asarray(place, jnp.bfloat16))


def unpack(x, wide, order):
    return pl.pallas_call(
        unpack_kernel,
        out_shape=jax.ShapeDtypeStruct((wide, order), jnp.bfloat16),
        compiler_params=pltpu.CompilerParams(vmem_limit_bytes=16 << 20),
        name="unpack",
    )(x)


def correlate(x):
    owners, here, lanes = x.shape[0], x.shape[1] // 5, x.shape[2]
    energies = owners * here
    points = energies * 2 // RADIX
    high, low, twiddle = tables(energies)
    return pl.pallas_call(
        correlate_kernel,
        out_shape=jax.ShapeDtypeStruct((owners, 2 * here, lanes), jnp.bfloat16),
        scratch_shapes=[
            pltpu.VMEM((4, 2, points, lanes), jnp.float32),
            pltpu.VMEM((2 * RADIX, points, lanes), jnp.float32),
        ],
        compiler_params=pltpu.CompilerParams(vmem_limit_bytes=24 << 20),
        name="correlate",
    )(x, jnp.asarray(high), jnp.asarray(low), jnp.asarray(twiddle))


def screen(polar, pieces, index, shape):
    energies, _, columns, order = shape
    out = pl.pallas_call(
        screen_kernel,
        out_shape=jax.ShapeDtypeStruct((energies * columns * order * 2 // LANES, LANES), jnp.float32),
        in_specs=[pl.BlockSpec(memory_space=pltpu.SMEM)]
        + [pl.BlockSpec(memory_space=pltpu.VMEM)] * (1 + len(pieces)),
        out_specs=pl.BlockSpec(memory_space=pltpu.VMEM),
        scratch_shapes=[pltpu.VMEM((len(pieces),) + pieces[0].shape, jnp.bfloat16)],
        compiler_params=pltpu.CompilerParams(vmem_limit_bytes=24 << 20),
        name="screen",
    )(index, polar, *pieces)
    out = out.reshape(energies, columns, order // LANES, 2, LANES).transpose(0, 1, 3, 2, 4)
    return out.reshape(energies, columns, 2, order).transpose(0, 2, 1, 3)


def moved(x, sharers, hops):
    def source(at):
        z, x, core = at // (ACROSS * CORES), at // CORES % ACROSS, at % CORES
        z, x, core = (z + hops[0]) % RUN, (x + hops[1]) % ACROSS, (core + hops[2]) % CORES
        return (z * ACROSS + x) * CORES + core

    return lax.ppermute(x, "col", [(source(at), at) for at in range(sharers)])


def per_device(lesser, greater_transposed, coulomb):
    owners = lax.axis_size("energy")
    sharers = lax.axis_size("col")
    order = lesser.shape[3]
    packed = pack(lesser, greater_transposed, coulomb, owners)
    got = lax.all_to_all(packed.astype(jnp.float16), "energy", split_axis=0, concat_axis=0, tiled=True)
    got = got.astype(jnp.float32)
    pieces = [unpack(got, coulomb.shape[1], order)]
    for axis, size in enumerate((RUN, ACROSS, CORES)):
        had = list(pieces)
        for hop in range(1, size):
            pieces += [moved(p, sharers, [hop * (axis == k) for k in range(3)]) for p in had]
    index = jnp.full((1,), lax.axis_index("col"), jnp.int32)
    polar = correlate(got)
    polar = lax.all_to_all(polar, "energy", split_axis=0, concat_axis=0, tiled=True)
    return screen(polar, pieces, index, lesser.shape)


def solution(mesh):
    placed = (P("energy", None, "col", None), P("energy", None, "col", None), P("energy", "col"))
    return jax.shard_map(
        per_device,
        mesh=mesh,
        in_specs=placed,
        out_specs=P("energy", None, "col", None),
        check_vma=False,
    )
```

```python
import functools
import math

import jax
import jax.numpy as jnp
import numpy as np
from jax import lax
from jax.experimental import pallas as pl
from jax.experimental.layout import Layout, with_layout_constraint
from jax.experimental.pallas import tpu as pltpu
from jax.sharding import PartitionSpec as P

LANES = 128
RADIX = 8
RUN, ACROSS, CORES = 3, 4, 2
HOPS = (0, 2, 1, 3)
HALF = math.sqrt(0.5)
COULOMB_SCALE = float(2**18)
SCALE = 4096.0


def split(x):
    high = x.astype(jnp.bfloat16)
    return high, (x - high.astype(jnp.float32)).astype(jnp.bfloat16)


def turn(re, im, eighths):
    eighths %= 8
    if eighths % 2:
        re, im = (re + im) * HALF, (im - re) * HALF
        eighths -= 1
    return ((re, im), (im, -re), (-re, -im), (-im, re))[eighths // 2]


def pack_kernel(lesser_hbm, greater_hbm, coulomb_hbm, out_ref, lesser_ref, greater_ref, coulomb_ref, sems):
    copies = [
        pltpu.make_async_copy(source, target, sems.at[i])
        for i, (source, target) in enumerate(
            ((lesser_hbm, lesser_ref), (greater_hbm, greater_ref), (coulomb_hbm, coulomb_ref))
        )
    ]
    for copy in copies:
        copy.start()
    here = out_ref.shape[1] // 5
    stride = lesser_ref.shape[0] // here
    blocks = stride // 2
    out_ref[blocks:, :4 * here, :] = jnp.zeros_like(out_ref[blocks:, :4 * here, :])
    for which, ref in enumerate((lesser_ref, greater_ref)):
        copies[which].wait()
        for block in range(blocks):
            for part in range(2):
                at = (which * 2 + part) * here
                out_ref[block, at:at + here, :] = ref[pl.ds(block * 2 + part, here, stride=stride), :] * SCALE
    copies[2].wait()
    block = coulomb_ref[...]
    rows, wide = block.shape
    row = lax.broadcasted_iota(jnp.int32, (rows, LANES), 0)
    lane = lax.broadcasted_iota(jnp.int32, (rows, LANES), 1)
    total = None
    for group in range(wide // here):
        place = jnp.where(lane == row + group * rows, COULOMB_SCALE, 0.0).astype(jnp.bfloat16)
        turned = lax.dot_general(block, place, (((0,), (0,)), ((), ())), preferred_element_type=jnp.float32)
        turned = turned[group * here:(group + 1) * here, :]
        total = turned if total is None else total + turned
    for owner in range(out_ref.shape[0]):
        out_ref[owner, 4 * here:, :] = total


def unpack_kernel(x_ref, out_ref):
    sources, rows, _ = x_ref.shape
    extra = rows // 5
    width = out_ref.shape[1] // sources
    for group in range(out_ref.shape[0] // extra):
        pieces = [
            x_ref[source, 4 * extra:, group * width:(group + 1) * width] for source in range(sources)
        ]
        row = jnp.concatenate(pieces, axis=1) * (1.0 / COULOMB_SCALE)
        out_ref[group * extra:(group + 1) * extra, :] = row.astype(jnp.bfloat16)


def correlate_kernel(x_ref, high_ref, low_ref, twiddle_ref, out_ref, total_ref, spread_ref):
    sources, here, lanes = x_ref.shape[0], x_ref.shape[1] // 5, x_ref.shape[2]
    points = high_ref.shape[0] // 2
    pieces = sources * here // points
    per_piece = sources // pieces
    high, low = high_ref[...], low_ref[...]

    def dft(re, im):
        x = jnp.concatenate([re, im], axis=0)
        x_high, x_low = split(x)
        y = jnp.dot(high, x_high, preferred_element_type=jnp.float32)
        y += jnp.dot(high, x_low, preferred_element_type=jnp.float32)
        return y + jnp.dot(low, x_high, preferred_element_type=jnp.float32)

    def piece(which, part, j):
        at = (which * 2 + part) * here
        return x_ref[j * per_piece:(j + 1) * per_piece, at:at + here, :].reshape(points, lanes)

    for r in range(RADIX // 2):
        for other in (r, r + RADIX // 2):
            spread_ref[2 * other] = jnp.broadcast_to(twiddle_ref[:, 2 * other:2 * other + 1], (points, lanes))
            spread_ref[2 * other + 1] = jnp.broadcast_to(twiddle_ref[:, 2 * other + 1:2 * other + 2], (points, lanes))
        sums = []
        for which in range(2):
            terms = []
            for j in range(4):
                re, im = piece(which, 0, j), piece(which, 1, j)
                if which:
                    im = -im
                terms.append(turn(re, im, r * j))
            even = [terms[0][k] + terms[2][k] for k in range(2)]
            odd = [terms[1][k] + terms[3][k] for k in range(2)]
            sums.append(([even[k] + odd[k] for k in range(2)], [even[k] - odd[k] for k in range(2)]))
        mixed = []
        for half, other in enumerate((r, r + RADIX // 2)):
            w_re, w_im = spread_ref[2 * other], spread_ref[2 * other + 1]
            turned = []
            for which in range(2):
                re, im = sums[which][half]
                turned.append((re * w_re - im * w_im, re * w_im + im * w_re))
            y = dft(
                jnp.concatenate([turned[0][0], turned[1][0]], axis=1),
                jnp.concatenate([turned[0][1], turned[1][1]], axis=1),
            )
            l_re, l_im = y[:points, :lanes], y[points:, :lanes]
            g_re, g_im = y[:points, lanes:], y[points:, lanes:]
            mixed.append((l_re * g_re + l_im * g_im, l_re * g_im - l_im * g_re))
        z = dft(
            jnp.concatenate([mixed[0][0], mixed[1][0]], axis=1),
            jnp.concatenate([mixed[0][1], mixed[1][1]], axis=1),
        )
        back = []
        for half, other in enumerate((r, r + RADIX // 2)):
            w_re, w_im = spread_ref[2 * other], spread_ref[2 * other + 1]
            re, im = z[:points, half * lanes:(half + 1) * lanes], z[points:, half * lanes:(half + 1) * lanes]
            back.append((re * w_re - im * w_im, re * w_im + im * w_re))
        both = [back[0][k] + back[1][k] for k in range(2)]
        apart = [back[0][k] - back[1][k] for k in range(2)]
        for j in range(4):
            re, im = turn(*(apart if j % 2 else both), r * j)
            if r == 0:
                total_ref[j, 0] = re
                total_ref[j, 1] = im
            else:
                total_ref[j, 0] += re
                total_ref[j, 1] += im
    energies = sources * here
    factor = -1.0 / (math.sqrt(energies) * 2 * energies * SCALE * SCALE)
    for j in range(pieces):
        for part in range(2):
            value = (total_ref[j, 1 - part] * factor).astype(jnp.bfloat16)
            out_ref[j * per_piece:(j + 1) * per_piece, part * here:(part + 1) * here, :] = value.reshape(
                per_piece, here, lanes
            )


def screen_kernel(place_ref, polar_ref, *refs):
    *run_refs, out_ref, coulomb_ref = refs
    run, wide, order = run_refs[0].shape
    across = len(run_refs) // CORES
    groups = order // LANES
    here = polar_ref.shape[1] // 2
    stride = out_ref.shape[0] // here
    columns = stride // 2 // groups
    z, x, core = place_ref[0], place_ref[1], place_ref[2]
    for at, hop_x in enumerate(HOPS):
        for hop in range(run):
            chip = lax.rem(z + hop, run) * across + lax.rem(x + hop_x, across)
            coulomb_ref[chip * CORES + core] = run_refs[at][hop]
            coulomb_ref[chip * CORES + 1 - core] = run_refs[across + at][hop]
    rows = [
        jnp.concatenate([polar_ref[c * groups + k] for k in range(groups)], axis=1) for c in range(columns)
    ]
    product = lax.dot_general(
        jnp.concatenate(rows, axis=0),
        coulomb_ref[...].reshape(order, order),
        (((1,), (1,)), ((), ())),
        preferred_element_type=jnp.float32,
    )
    for c in range(columns):
        for part in range(2):
            at = (c * 2 + part) * here
            for k in range(groups):
                out_ref[pl.ds((c * groups + k) * 2 + part, here, stride=stride), :] = product[
                    at:at + here, k * LANES:(k + 1) * LANES
                ]


def tables(energies):
    points = energies * 2 // RADIX
    angle = np.outer(np.arange(points), np.arange(points)) % points * (2 * np.pi / points)
    cos, sin = np.cos(angle), np.sin(angle)
    whole = np.block([[cos, sin], [-sin, cos]])
    high = whole.astype(jnp.bfloat16)
    low = (whole - high.astype(np.float64)).astype(jnp.bfloat16)
    twiddle = np.zeros((points, LANES), np.float32)
    for r in range(RADIX):
        turned = np.arange(points) * r * (np.pi / energies)
        twiddle[:, 2 * r], twiddle[:, 2 * r + 1] = np.cos(turned), -np.sin(turned)
    return high, low, twiddle


def rows_view(x):
    energies, _, columns, order = x.shape
    x = x.reshape(energies, 2, columns, order // LANES, LANES).transpose(0, 2, 3, 1, 4)
    x = with_layout_constraint(x, Layout(tuple(range(x.ndim))))
    return x.reshape(-1, LANES)


def pack(lesser, greater, coulomb, owners):
    here = lesser.shape[0]
    lesser, greater = rows_view(lesser), rows_view(greater)
    return pl.pallas_call(
        pack_kernel,
        out_shape=jax.ShapeDtypeStruct((owners, 5 * here, LANES), jnp.float32),
        in_specs=[pl.BlockSpec(memory_space=pltpu.HBM)] * 3,
        out_specs=pl.BlockSpec(memory_space=pltpu.VMEM),
        scratch_shapes=[pltpu.VMEM(x.shape, x.dtype) for x in (lesser, greater, coulomb)]
        + [pltpu.SemaphoreType.DMA((3,))],
        compiler_params=pltpu.CompilerParams(vmem_limit_bytes=16 << 20),
        name="pack",
    )(*(pltpu.with_memory_space_constraint(x, pltpu.HBM) for x in (lesser, greater, coulomb)))


def unpack(x, wide, order):
    return pl.pallas_call(
        unpack_kernel,
        out_shape=jax.ShapeDtypeStruct((wide, order), jnp.bfloat16),
        compiler_params=pltpu.CompilerParams(vmem_limit_bytes=16 << 20),
        name="unpack",
    )(x)


def correlate(x):
    owners, here, lanes = x.shape[0], x.shape[1] // 5, x.shape[2]
    energies = owners * here
    points = energies * 2 // RADIX
    high, low, twiddle = tables(energies)
    return pl.pallas_call(
        correlate_kernel,
        out_shape=jax.ShapeDtypeStruct((owners, 2 * here, lanes), jnp.bfloat16),
        scratch_shapes=[
            pltpu.VMEM((4, 2, points, lanes), jnp.float32),
            pltpu.VMEM((2 * RADIX, points, lanes), jnp.float32),
        ],
        compiler_params=pltpu.CompilerParams(vmem_limit_bytes=24 << 20),
        cost_estimate=pl.CostEstimate(
            flops=RADIX * 3 * 2 * (2 * points) ** 2 * 3 * lanes, bytes_accessed=x.size * 4 + x.size, transcendentals=0
        ),
        name="correlate",
    )(x, jnp.asarray(high), jnp.asarray(low), jnp.asarray(twiddle))


def screen(polar, runs, place, shape):
    energies, _, columns, order = shape
    run, wide, _ = runs[0].shape
    out = pl.pallas_call(
        screen_kernel,
        out_shape=jax.ShapeDtypeStruct((energies * columns * order * 2 // LANES, LANES), jnp.float32),
        in_specs=[pl.BlockSpec(memory_space=pltpu.SMEM)]
        + [pl.BlockSpec(memory_space=pltpu.VMEM)] * (1 + len(runs)),
        out_specs=pl.BlockSpec(memory_space=pltpu.VMEM),
        scratch_shapes=[pltpu.VMEM((len(runs) * run, wide, order), jnp.bfloat16)],
        compiler_params=pltpu.CompilerParams(vmem_limit_bytes=24 << 20),
        name="screen",
    )(place, polar, *runs)
    out = out.reshape(energies, columns, order // LANES, 2, LANES).transpose(0, 1, 3, 2, 4)
    return out.reshape(energies, columns, 2, order).transpose(0, 2, 1, 3)


def moved(x, sharers, hops):
    def source(at):
        z, x, core = at // (ACROSS * CORES), at // CORES % ACROSS, at % CORES
        z, x, core = (z + hops[0]) % RUN, (x + hops[1]) % ACROSS, (core + hops[2]) % CORES
        return (z * ACROSS + x) * CORES + core

    return lax.ppermute(x, "col", [(source(at), at) for at in range(sharers)])


def per_device(lesser, greater_transposed, coulomb):
    owners = lax.axis_size("energy")
    sharers = lax.axis_size("col")
    order = lesser.shape[3]
    packed = pack(lesser, greater_transposed, coulomb, owners)
    got = lax.all_to_all(packed.astype(jnp.float16), "energy", split_axis=0, concat_axis=0, tiled=True)
    got = got.astype(jnp.float32)
    wide = coulomb.shape[1]
    mine = unpack(got, wide, order)
    run = jnp.stack([mine] + [moved(mine, sharers, (hop, 0, 0)) for hop in range(1, RUN)])
    polar = correlate(got)
    run, polar = lax.optimization_barrier((run, polar))
    runs = [run] + [moved(run, sharers, (0, hop, 0)) for hop in HOPS[1:]]
    runs += [moved(run, sharers, (0, 0, 1)) for run in runs]
    polar = lax.all_to_all(polar, "energy", split_axis=0, concat_axis=0, tiled=True)
    at = lax.axis_index("col")
    place = [lax.div(at, ACROSS * CORES), lax.rem(lax.div(at, CORES), ACROSS), lax.rem(at, CORES)]
    return screen(polar, runs, jnp.stack(place).astype(jnp.int32), lesser.shape)


def solution(mesh):
    placed = (P("energy", None, "col", None), P("energy", None, "col", None), P("energy", "col"))
    return jax.shard_map(
        per_device,
        mesh=mesh,
        in_specs=placed,
        out_specs=P("energy", None, "col", None),
        check_vma=False,
    )
```

```python
import functools
import math

import jax
import jax.numpy as jnp
import numpy as np
from jax import lax
from jax.experimental import pallas as pl
from jax.experimental.layout import Layout, with_layout_constraint
from jax.experimental.pallas import tpu as pltpu
from jax.sharding import PartitionSpec as P

LANES = 128
RADIX = 8
PARTS = 4
RUN, ACROSS, CORES = 3, 4, 2
HOPS = (0, 1, 3, 2)
HALF = math.sqrt(0.5)
COULOMB_SCALE = float(2**18)
SCALE = 4096.0


def split(x):
    high = x.astype(jnp.bfloat16)
    return high, (x - high.astype(jnp.float32)).astype(jnp.bfloat16)


def turn(re, im, eighths):
    eighths %= 8
    if eighths % 2:
        re, im = (re + im) * HALF, (im - re) * HALF
        eighths -= 1
    return ((re, im), (im, -re), (-re, -im), (-im, re))[eighths // 2]


def pack_kernel(lesser_hbm, greater_hbm, coulomb_hbm, out_ref, lesser_ref, greater_ref, coulomb_ref, sems):
    copies = []
    for which, (source, target) in enumerate(((lesser_hbm, lesser_ref), (greater_hbm, greater_ref))):
        rows = source.shape[0] // PARTS
        for part in range(PARTS):
            at = pl.ds(part * rows, rows)
            copies.append(pltpu.make_async_copy(source.at[at, :], target.at[at, :], sems.at[which * PARTS + part]))
    copies.append(pltpu.make_async_copy(coulomb_hbm, coulomb_ref, sems.at[2 * PARTS]))
    for copy in copies:
        copy.start()
    here = out_ref.shape[1] // 5
    stride = lesser_ref.shape[0] // here
    blocks = stride // 2
    out_ref[blocks:, :4 * here, :] = jnp.zeros_like(out_ref[blocks:, :4 * here, :])
    for which, ref in enumerate((lesser_ref, greater_ref)):
        for copy in copies[which * PARTS:(which + 1) * PARTS]:
            copy.wait()
        for block in range(blocks):
            for part in range(2):
                at = (which * 2 + part) * here
                out_ref[block, at:at + here, :] = ref[pl.ds(block * 2 + part, here, stride=stride), :] * SCALE
    copies[2 * PARTS].wait()
    block = coulomb_ref[...]
    rows, wide = block.shape
    row = lax.broadcasted_iota(jnp.int32, (rows, LANES), 0)
    lane = lax.broadcasted_iota(jnp.int32, (rows, LANES), 1)
    total = None
    for group in range(wide // here):
        place = jnp.where(lane == row + group * rows, COULOMB_SCALE, 0.0).astype(jnp.bfloat16)
        turned = lax.dot_general(block, place, (((0,), (0,)), ((), ())), preferred_element_type=jnp.float32)
        turned = turned[group * here:(group + 1) * here, :]
        total = turned if total is None else total + turned
    for owner in range(out_ref.shape[0]):
        out_ref[owner, 4 * here:, :] = total


def unpack_kernel(x_ref, out_ref):
    sources, rows, _ = x_ref.shape
    extra = rows // 5
    width = out_ref.shape[1] // sources
    for group in range(out_ref.shape[0] // extra):
        pieces = [
            x_ref[source, 4 * extra:, group * width:(group + 1) * width] for source in range(sources)
        ]
        row = jnp.concatenate(pieces, axis=1) * (1.0 / COULOMB_SCALE)
        out_ref[group * extra:(group + 1) * extra, :] = row.astype(jnp.bfloat16)


def correlate_kernel(x_ref, matrices_ref, twiddle_ref, out_ref, total_ref, spread_ref):
    sources, here, lanes = x_ref.shape[0], x_ref.shape[1] // 5, x_ref.shape[2]
    rows = matrices_ref.shape[1]
    points = rows // 2
    pieces = sources * here // points
    per_piece = sources // pieces
    matrices = matrices_ref[...]

    def dft(re, im):
        x = jnp.concatenate([re, im], axis=0)
        x_high, x_low = split(x)
        both = jnp.dot(matrices, x_high, preferred_element_type=jnp.float32)
        return both[:rows] + both[rows:] + jnp.dot(matrices[:rows], x_low, preferred_element_type=jnp.float32)

    def piece(which, part, j):
        at = (which * 2 + part) * here
        return x_ref[j * per_piece:(j + 1) * per_piece, at:at + here, :].reshape(points, lanes)

    for r in range(RADIX // 2):
        for other in (r, r + RADIX // 2):
            spread_ref[2 * other] = jnp.broadcast_to(twiddle_ref[:, 2 * other:2 * other + 1], (points, lanes))
            spread_ref[2 * other + 1] = jnp.broadcast_to(twiddle_ref[:, 2 * other + 1:2 * other + 2], (points, lanes))
        sums = []
        for which in range(2):
            terms = []
            for j in range(4):
                re, im = piece(which, 0, j), piece(which, 1, j)
                if which:
                    im = -im
                terms.append(turn(re, im, r * j))
            even = [terms[0][k] + terms[2][k] for k in range(2)]
            odd = [terms[1][k] + terms[3][k] for k in range(2)]
            sums.append(([even[k] + odd[k] for k in range(2)], [even[k] - odd[k] for k in range(2)]))
        mixed = []
        for half, other in enumerate((r, r + RADIX // 2)):
            w_re, w_im = spread_ref[2 * other], spread_ref[2 * other + 1]
            turned = []
            for which in range(2):
                re, im = sums[which][half]
                turned.append((re * w_re - im * w_im, re * w_im + im * w_re))
            y = dft(
                jnp.concatenate([turned[0][0], turned[1][0]], axis=1),
                jnp.concatenate([turned[0][1], turned[1][1]], axis=1),
            )
            l_re, l_im = y[:points, :lanes], y[points:, :lanes]
            g_re, g_im = y[:points, lanes:], y[points:, lanes:]
            mixed.append((l_re * g_re + l_im * g_im, l_re * g_im - l_im * g_re))
        z = dft(
            jnp.concatenate([mixed[0][0], mixed[1][0]], axis=1),
            jnp.concatenate([mixed[0][1], mixed[1][1]], axis=1),
        )
        back = []
        for half, other in enumerate((r, r + RADIX // 2)):
            w_re, w_im = spread_ref[2 * other], spread_ref[2 * other + 1]
            re, im = z[:points, half * lanes:(half + 1) * lanes], z[points:, half * lanes:(half + 1) * lanes]
            back.append((re * w_re - im * w_im, re * w_im + im * w_re))
        both = [back[0][k] + back[1][k] for k in range(2)]
        apart = [back[0][k] - back[1][k] for k in range(2)]
        for j in range(4):
            re, im = turn(*(apart if j % 2 else both), r * j)
            if r == 0:
                total_ref[j, 0] = re
                total_ref[j, 1] = im
            else:
                total_ref[j, 0] += re
                total_ref[j, 1] += im
    energies = sources * here
    factor = -1.0 / (math.sqrt(energies) * 2 * energies * SCALE * SCALE)
    for j in range(pieces):
        for part in range(2):
            value = (total_ref[j, 1 - part] * factor).astype(jnp.bfloat16)
            out_ref[j * per_piece:(j + 1) * per_piece, part * here:(part + 1) * here, :] = value.reshape(
                per_piece, here, lanes
            )


def product_kernel(place_ref, polar_ref, *refs):
    *run_refs, out_ref, coulomb_ref = refs
    run, wide, order = run_refs[0].shape
    across = len(run_refs)
    groups = order // LANES
    z, x = place_ref[0], place_ref[1]
    for at, hop_x in enumerate(HOPS):
        for hop in range(run):
            coulomb_ref[lax.rem(z + hop, run) * across + lax.rem(x + hop_x, across)] = run_refs[at][hop]
    columns = out_ref.shape[0] // polar_ref.shape[1]
    rows = [
        jnp.concatenate([polar_ref[c * groups + k] for k in range(groups)], axis=1) for c in range(columns)
    ]
    out_ref[...] = lax.dot_general(
        jnp.concatenate(rows, axis=0),
        coulomb_ref[...].reshape(across * run * wide, order),
        (((1,), (1,)), ((), ())),
        preferred_element_type=jnp.float32,
    )


def merge_kernel(place_ref, mine_ref, other_ref, out_ref, *, wide, here):
    first = place_ref[2] == 0
    stride = out_ref.shape[0] // here
    columns = mine_ref.shape[0] // (2 * here)
    for at in range(columns * 2):
        rows = slice(at * here, (at + 1) * here)
        mine, other = mine_ref[rows, :], other_ref[rows, :]
        cores = jnp.where(first, mine, other), jnp.where(first, other, mine)
        pieces = []
        for chip in range(mine.shape[1] // wide):
            pieces += [part[:, chip * wide:(chip + 1) * wide] for part in cores]
        row = jnp.concatenate(pieces, axis=1)
        groups = row.shape[1] // LANES
        for k in range(groups):
            out_ref[pl.ds((at // 2 * groups + k) * 2 + at % 2, here, stride=stride), :] = row[
                :, k * LANES:(k + 1) * LANES
            ]


def tables(energies):
    points = energies * 2 // RADIX
    angle = np.outer(np.arange(points), np.arange(points)) % points * (2 * np.pi / points)
    cos, sin = np.cos(angle), np.sin(angle)
    whole = np.block([[cos, sin], [-sin, cos]])
    high = whole.astype(jnp.bfloat16)
    low = (whole - high.astype(np.float64)).astype(jnp.bfloat16)
    twiddle = np.zeros((points, LANES), np.float32)
    for r in range(RADIX):
        turned = np.arange(points) * r * (np.pi / energies)
        twiddle[:, 2 * r], twiddle[:, 2 * r + 1] = np.cos(turned), -np.sin(turned)
    return np.concatenate([high, low]), twiddle


def rows_view(x):
    energies, _, columns, order = x.shape
    x = x.reshape(energies, 2, columns, order // LANES, LANES).transpose(0, 2, 3, 1, 4)
    x = with_layout_constraint(x, Layout(tuple(range(x.ndim))))
    return x.reshape(-1, LANES)


def pack(lesser, greater, coulomb, owners):
    here = lesser.shape[0]
    lesser, greater = rows_view(lesser), rows_view(greater)
    return pl.pallas_call(
        pack_kernel,
        out_shape=jax.ShapeDtypeStruct((owners, 5 * here, LANES), jnp.float32),
        in_specs=[pl.BlockSpec(memory_space=pltpu.HBM)] * 3,
        out_specs=pl.BlockSpec(memory_space=pltpu.VMEM),
        scratch_shapes=[pltpu.VMEM(x.shape, x.dtype) for x in (lesser, greater, coulomb)]
        + [pltpu.SemaphoreType.DMA((2 * PARTS + 1,))],
        compiler_params=pltpu.CompilerParams(vmem_limit_bytes=16 << 20),
        name="pack",
    )(*(pltpu.with_memory_space_constraint(x, pltpu.HBM) for x in (lesser, greater, coulomb)))


def unpack(x, wide, order):
    return pl.pallas_call(
        unpack_kernel,
        out_shape=jax.ShapeDtypeStruct((wide, order), jnp.bfloat16),
        compiler_params=pltpu.CompilerParams(vmem_limit_bytes=16 << 20),
        name="unpack",
    )(x)


def correlate(x):
    owners, here, lanes = x.shape[0], x.shape[1] // 5, x.shape[2]
    energies = owners * here
    points = energies * 2 // RADIX
    matrices, twiddle = tables(energies)
    return pl.pallas_call(
        correlate_kernel,
        out_shape=jax.ShapeDtypeStruct((owners, 2 * here, lanes), jnp.bfloat16),
        scratch_shapes=[
            pltpu.VMEM((4, 2, points, lanes), jnp.float32),
            pltpu.VMEM((2 * RADIX, points, lanes), jnp.float32),
        ],
        compiler_params=pltpu.CompilerParams(vmem_limit_bytes=24 << 20),
        cost_estimate=pl.CostEstimate(
            flops=RADIX * 3 * 2 * (2 * points) ** 2 * 3 * lanes, bytes_accessed=x.size * 4 + x.size, transcendentals=0
        ),
        name="correlate",
    )(x, jnp.asarray(matrices), jnp.asarray(twiddle))


def product(polar, runs, place, columns):
    run, wide, order = runs[0].shape
    chips = len(runs) * run
    return pl.pallas_call(
        product_kernel,
        out_shape=jax.ShapeDtypeStruct((columns * polar.shape[1], chips * wide), jnp.float32),
        in_specs=[pl.BlockSpec(memory_space=pltpu.SMEM)]
        + [pl.BlockSpec(memory_space=pltpu.VMEM)] * (1 + len(runs)),
        out_specs=pl.BlockSpec(memory_space=pltpu.VMEM),
        scratch_shapes=[pltpu.VMEM((chips, wide, order), jnp.bfloat16)],
        compiler_params=pltpu.CompilerParams(vmem_limit_bytes=24 << 20),
        name="product",
    )(place, polar, *runs)


def merge(mine, other, place, wide, shape):
    energies, _, columns, order = shape
    out = pl.pallas_call(
        functools.partial(merge_kernel, wide=wide, here=energies),
        out_shape=jax.ShapeDtypeStruct((energies * columns * order * 2 // LANES, LANES), jnp.float32),
        in_specs=[pl.BlockSpec(memory_space=pltpu.SMEM)] + [pl.BlockSpec(memory_space=pltpu.VMEM)] * 2,
        out_specs=pl.BlockSpec(memory_space=pltpu.VMEM),
        compiler_params=pltpu.CompilerParams(vmem_limit_bytes=16 << 20),
        name="merge",
    )(place, mine, other)
    out = out.reshape(energies, columns, order // LANES, 2, LANES).transpose(0, 1, 3, 2, 4)
    return out.reshape(energies, columns, 2, order).transpose(0, 2, 1, 3)


def moved(x, sharers, hops):
    def source(at):
        z, x, core = at // (ACROSS * CORES), at // CORES % ACROSS, at % CORES
        z, x, core = (z + hops[0]) % RUN, (x + hops[1]) % ACROSS, (core + hops[2]) % CORES
        return (z * ACROSS + x) * CORES + core

    return lax.ppermute(x, "col", [(source(at), at) for at in range(sharers)])


def per_device(lesser, greater_transposed, coulomb):
    owners = lax.axis_size("energy")
    sharers = lax.axis_size("col")
    order = lesser.shape[3]
    packed = pack(lesser, greater_transposed, coulomb, owners)
    got = lax.all_to_all(packed.astype(jnp.float16), "energy", split_axis=0, concat_axis=0, tiled=True)
    got = got.astype(jnp.float32)
    wide = coulomb.shape[1]
    mine = unpack(got, wide, order)
    run = jnp.stack([mine] + [moved(mine, sharers, (hop, 0, 0)) for hop in range(1, RUN)])
    polar = correlate(got)
    run, polar = lax.optimization_barrier((run, polar))
    runs = [run] + [moved(run, sharers, (0, hop, 0)) for hop in HOPS[1:]]
    polar = lax.all_to_all(polar, "energy", split_axis=0, concat_axis=0, tiled=True)
    at = lax.axis_index("col")
    place = [lax.div(at, ACROSS * CORES), lax.rem(lax.div(at, CORES), ACROSS), lax.rem(at, CORES)]
    place = jnp.stack(place).astype(jnp.int32)
    given = product(moved(polar, sharers, (0, 0, 1)), runs, place, lesser.shape[2])
    other = moved(given, sharers, (0, 0, 1))
    return merge(product(polar, runs, place, lesser.shape[2]), other, place, coulomb.shape[1], lesser.shape)


def solution(mesh):
    placed = (P("energy", None, "col", None), P("energy", None, "col", None), P("energy", "col"))
    return jax.shard_map(
        per_device,
        mesh=mesh,
        in_specs=placed,
        out_specs=P("energy", None, "col", None),
        check_vma=False,
    )
```

```python
import functools
import math

import jax
import jax.numpy as jnp
import numpy as np
from jax import lax
from jax.experimental import pallas as pl
from jax.experimental.layout import Layout, with_layout_constraint
from jax.experimental.pallas import tpu as pltpu
from jax.sharding import PartitionSpec as P

LANES = 128
RADIX = 8
RUN, ACROSS, CORES = 3, 4, 2
HOPS = (0, 1, 3, 2)
HALF = math.sqrt(0.5)
COULOMB_SCALE = float(2**18)
SCALE = 4096.0


def split(x):
    high = x.astype(jnp.bfloat16)
    return high, (x - high.astype(jnp.float32)).astype(jnp.bfloat16)


def turn(re, im, eighths):
    eighths %= 8
    if eighths % 2:
        re, im = (re + im) * HALF, (im - re) * HALF
        eighths -= 1
    return ((re, im), (im, -re), (-re, -im), (-im, re))[eighths // 2]


def pack_kernel(lesser_hbm, greater_hbm, coulomb_hbm, out_ref, lesser_ref, greater_ref, coulomb_ref, sems):
    copies = [
        pltpu.make_async_copy(source, target, sems.at[i])
        for i, (source, target) in enumerate(
            ((lesser_hbm, lesser_ref), (greater_hbm, greater_ref), (coulomb_hbm, coulomb_ref))
        )
    ]
    for copy in copies:
        copy.start()
    here = out_ref.shape[1] // 5
    stride = lesser_ref.shape[0] // here
    blocks = stride // 2
    out_ref[blocks:, :4 * here, :] = jnp.zeros_like(out_ref[blocks:, :4 * here, :])
    for which, ref in enumerate((lesser_ref, greater_ref)):
        copies[which].wait()
        for block in range(blocks):
            for part in range(2):
                at = (which * 2 + part) * here
                out_ref[block, at:at + here, :] = ref[pl.ds(block * 2 + part, here, stride=stride), :] * SCALE
    copies[2].wait()
    block = coulomb_ref[...]
    rows, wide = block.shape
    row = lax.broadcasted_iota(jnp.int32, (rows, LANES), 0)
    lane = lax.broadcasted_iota(jnp.int32, (rows, LANES), 1)
    total = None
    for group in range(wide // here):
        place = jnp.where(lane == row + group * rows, COULOMB_SCALE, 0.0).astype(jnp.bfloat16)
        turned = lax.dot_general(block, place, (((0,), (0,)), ((), ())), preferred_element_type=jnp.float32)
        turned = turned[group * here:(group + 1) * here, :]
        total = turned if total is None else total + turned
    for owner in range(out_ref.shape[0]):
        out_ref[owner, 4 * here:, :] = total


def unpack_kernel(x_ref, out_ref):
    sources, rows, _ = x_ref.shape
    extra = rows // 5
    width = out_ref.shape[1] // sources
    for group in range(out_ref.shape[0] // extra):
        pieces = [
            x_ref[source, 4 * extra:, group * width:(group + 1) * width] for source in range(sources)
        ]
        row = jnp.concatenate(pieces, axis=1) * (1.0 / COULOMB_SCALE)
        out_ref[group * extra:(group + 1) * extra, :] = row.astype(jnp.bfloat16)


def correlate_kernel(x_ref, matrices_ref, twiddle_ref, out_ref, total_ref, spread_ref):
    sources, here, lanes = x_ref.shape[0], x_ref.shape[1] // 5, x_ref.shape[2]
    rows = matrices_ref.shape[1]
    points = rows // 2
    pieces = sources * here // points
    per_piece = sources // pieces
    matrices = matrices_ref[...]

    def dft(re, im):
        x = jnp.concatenate([re, im], axis=0)
        x_high, x_low = split(x)
        both = jnp.dot(matrices, x_high, preferred_element_type=jnp.float32)
        return both[:rows] + both[rows:] + jnp.dot(matrices[:rows], x_low, preferred_element_type=jnp.float32)

    def piece(which, part, j):
        at = (which * 2 + part) * here
        return x_ref[j * per_piece:(j + 1) * per_piece, at:at + here, :].reshape(points, lanes)

    for r in range(RADIX // 2):
        for other in (r, r + RADIX // 2):
            spread_ref[2 * other] = jnp.broadcast_to(twiddle_ref[:, 2 * other:2 * other + 1], (points, lanes))
            spread_ref[2 * other + 1] = jnp.broadcast_to(twiddle_ref[:, 2 * other + 1:2 * other + 2], (points, lanes))
        sums = []
        for which in range(2):
            terms = []
            for j in range(4):
                re, im = piece(which, 0, j), piece(which, 1, j)
                if which:
                    im = -im
                terms.append(turn(re, im, r * j))
            even = [terms[0][k] + terms[2][k] for k in range(2)]
            odd = [terms[1][k] + terms[3][k] for k in range(2)]
            sums.append(([even[k] + odd[k] for k in range(2)], [even[k] - odd[k] for k in range(2)]))
        mixed = []
        for half, other in enumerate((r, r + RADIX // 2)):
            w_re, w_im = spread_ref[2 * other], spread_ref[2 * other + 1]
            turned = []
            for which in range(2):
                re, im = sums[which][half]
                turned.append((re * w_re - im * w_im, re * w_im + im * w_re))
            y = dft(
                jnp.concatenate([turned[0][0], turned[1][0]], axis=1),
                jnp.concatenate([turned[0][1], turned[1][1]], axis=1),
            )
            l_re, l_im = y[:points, :lanes], y[points:, :lanes]
            g_re, g_im = y[:points, lanes:], y[points:, lanes:]
            mixed.append((l_re * g_re + l_im * g_im, l_re * g_im - l_im * g_re))
        z = dft(
            jnp.concatenate([mixed[0][0], mixed[1][0]], axis=1),
            jnp.concatenate([mixed[0][1], mixed[1][1]], axis=1),
        )
        back = []
        for half, other in enumerate((r, r + RADIX // 2)):
            w_re, w_im = spread_ref[2 * other], spread_ref[2 * other + 1]
            re, im = z[:points, half * lanes:(half + 1) * lanes], z[points:, half * lanes:(half + 1) * lanes]
            back.append((re * w_re - im * w_im, re * w_im + im * w_re))
        both = [back[0][k] + back[1][k] for k in range(2)]
        apart = [back[0][k] - back[1][k] for k in range(2)]
        for j in range(4):
            re, im = turn(*(apart if j % 2 else both), r * j)
            if r == 0:
                total_ref[j, 0] = re
                total_ref[j, 1] = im
            else:
                total_ref[j, 0] += re
                total_ref[j, 1] += im
    energies = sources * here
    factor = -1.0 / (math.sqrt(energies) * 2 * energies * SCALE * SCALE)
    for j in range(pieces):
        for part in range(2):
            value = (total_ref[j, 1 - part] * factor).astype(jnp.bfloat16)
            out_ref[j * per_piece:(j + 1) * per_piece, part * here:(part + 1) * here, :] = value.reshape(
                per_piece, here, lanes
            )


def screen_kernel(place_ref, polar_ref, *refs):
    *run_refs, out_ref, coulomb_ref = refs
    run, wide, order = run_refs[0].shape
    across = len(run_refs) // CORES
    groups = order // LANES
    here = polar_ref.shape[1] // 2
    stride = out_ref.shape[0] // here
    columns = stride // 2 // groups
    z, x, core = place_ref[0], place_ref[1], place_ref[2]
    for at, hop_x in enumerate(HOPS):
        for hop in range(run):
            chip = lax.rem(z + hop, run) * across + lax.rem(x + hop_x, across)
            coulomb_ref[chip * CORES + core] = run_refs[at][hop]
            coulomb_ref[chip * CORES + 1 - core] = run_refs[across + at][hop]
    rows = [
        jnp.concatenate([polar_ref[c * groups + k] for k in range(groups)], axis=1) for c in range(columns)
    ]
    product = lax.dot_general(
        jnp.concatenate(rows, axis=0),
        coulomb_ref[...].reshape(order, order),
        (((1,), (1,)), ((), ())),
        preferred_element_type=jnp.float32,
    )
    for c in range(columns):
        for part in range(2):
            at = (c * 2 + part) * here
            for k in range(groups):
                out_ref[pl.ds((c * groups + k) * 2 + part, here, stride=stride), :] = product[
                    at:at + here, k * LANES:(k + 1) * LANES
                ]


def tables(energies):
    points = energies * 2 // RADIX
    angle = np.outer(np.arange(points), np.arange(points)) % points * (2 * np.pi / points)
    cos, sin = np.cos(angle), np.sin(angle)
    whole = np.block([[cos, sin], [-sin, cos]])
    high = whole.astype(jnp.bfloat16)
    low = (whole - high.astype(np.float64)).astype(jnp.bfloat16)
    twiddle = np.zeros((points, LANES), np.float32)
    for r in range(RADIX):
        turned = np.arange(points) * r * (np.pi / energies)
        twiddle[:, 2 * r], twiddle[:, 2 * r + 1] = np.cos(turned), -np.sin(turned)
    return np.concatenate([high, low]), twiddle


def rows_view(x):
    energies, _, columns, order = x.shape
    x = x.reshape(energies, 2, columns, order // LANES, LANES).transpose(0, 2, 3, 1, 4)
    x = with_layout_constraint(x, Layout(tuple(range(x.ndim))))
    return x.reshape(-1, LANES)


def pack(lesser, greater, coulomb, owners):
    here = lesser.shape[0]
    lesser, greater = rows_view(lesser), rows_view(greater)
    return pl.pallas_call(
        pack_kernel,
        out_shape=jax.ShapeDtypeStruct((owners, 5 * here, LANES), jnp.float32),
        in_specs=[pl.BlockSpec(memory_space=pltpu.HBM)] * 3,
        out_specs=pl.BlockSpec(memory_space=pltpu.VMEM),
        scratch_shapes=[pltpu.VMEM(x.shape, x.dtype) for x in (lesser, greater, coulomb)]
        + [pltpu.SemaphoreType.DMA((3,))],
        compiler_params=pltpu.CompilerParams(vmem_limit_bytes=16 << 20),
        name="pack",
    )(*(pltpu.with_memory_space_constraint(x, pltpu.HBM) for x in (lesser, greater, coulomb)))


def unpack(x, wide, order):
    return pl.pallas_call(
        unpack_kernel,
        out_shape=jax.ShapeDtypeStruct((wide, order), jnp.bfloat16),
        compiler_params=pltpu.CompilerParams(vmem_limit_bytes=16 << 20),
        name="unpack",
    )(x)


def correlate(x):
    owners, here, lanes = x.shape[0], x.shape[1] // 5, x.shape[2]
    energies = owners * here
    points = energies * 2 // RADIX
    matrices, twiddle = tables(energies)
    return pl.pallas_call(
        correlate_kernel,
        out_shape=jax.ShapeDtypeStruct((owners, 2 * here, lanes), jnp.bfloat16),
        scratch_shapes=[
            pltpu.VMEM((4, 2, points, lanes), jnp.float32),
            pltpu.VMEM((2 * RADIX, points, lanes), jnp.float32),
        ],
        compiler_params=pltpu.CompilerParams(vmem_limit_bytes=24 << 20),
        cost_estimate=pl.CostEstimate(
            flops=RADIX * 3 * 2 * (2 * points) ** 2 * 3 * lanes, bytes_accessed=x.size * 4 + x.size, transcendentals=0
        ),
        name="correlate",
    )(x, jnp.asarray(matrices), jnp.asarray(twiddle))


def screen(polar, runs, place, shape):
    energies, _, columns, order = shape
    run, wide, _ = runs[0].shape
    out = pl.pallas_call(
        screen_kernel,
        out_shape=jax.ShapeDtypeStruct((energies * columns * order * 2 // LANES, LANES), jnp.float32),
        in_specs=[pl.BlockSpec(memory_space=pltpu.SMEM)]
        + [pl.BlockSpec(memory_space=pltpu.VMEM)] * (1 + len(runs)),
        out_specs=pl.BlockSpec(memory_space=pltpu.VMEM),
        scratch_shapes=[pltpu.VMEM((len(runs) * run, wide, order), jnp.bfloat16)],
        compiler_params=pltpu.CompilerParams(vmem_limit_bytes=24 << 20),
        name="screen",
    )(place, polar, *runs)
    out = out.reshape(energies, columns, order // LANES, 2, LANES).transpose(0, 1, 3, 2, 4)
    return out.reshape(energies, columns, 2, order).transpose(0, 2, 1, 3)


def moved(x, sharers, hops):
    def source(at):
        z, x, core = at // (ACROSS * CORES), at // CORES % ACROSS, at % CORES
        z, x, core = (z + hops[0]) % RUN, (x + hops[1]) % ACROSS, (core + hops[2]) % CORES
        return (z * ACROSS + x) * CORES + core

    return lax.ppermute(x, "col", [(source(at), at) for at in range(sharers)])


def per_device(lesser, greater_transposed, coulomb):
    owners = lax.axis_size("energy")
    sharers = lax.axis_size("col")
    order = lesser.shape[3]
    packed = pack(lesser, greater_transposed, coulomb, owners)
    got = lax.all_to_all(packed.astype(jnp.float16), "energy", split_axis=0, concat_axis=0, tiled=True)
    got = got.astype(jnp.float32)
    wide = coulomb.shape[1]
    mine = unpack(got, wide, order)
    run = jnp.stack([mine] + [moved(mine, sharers, (hop, 0, 0)) for hop in range(1, RUN)])
    polar = correlate(got)
    run, polar = lax.optimization_barrier((run, polar))
    runs = [run] + [moved(run, sharers, (0, hop, 0)) for hop in HOPS[1:]]
    runs += [moved(run, sharers, (0, 0, 1)) for run in runs]
    polar = lax.all_to_all(polar, "energy", split_axis=0, concat_axis=0, tiled=True)
    at = lax.axis_index("col")
    place = [lax.div(at, ACROSS * CORES), lax.rem(lax.div(at, CORES), ACROSS), lax.rem(at, CORES)]
    return screen(polar, runs, jnp.stack(place).astype(jnp.int32), lesser.shape)


def solution(mesh):
    placed = (P("energy", None, "col", None), P("energy", None, "col", None), P("energy", "col"))
    return jax.shard_map(
        per_device,
        mesh=mesh,
        in_specs=placed,
        out_specs=P("energy", None, "col", None),
        check_vma=False,
    )
```

```python
import functools
import math

import jax
import jax.numpy as jnp
import numpy as np
from jax import lax
from jax.experimental import pallas as pl
from jax.experimental.layout import Layout, with_layout_constraint
from jax.experimental.pallas import tpu as pltpu
from jax.sharding import PartitionSpec as P

LANES = 128
RADIX = 8
APART = 4
RUN, ACROSS, CORES = 3, 4, 2
HOPS = (0, 1, 3, 2)
HALF = math.sqrt(0.5)
COULOMB_SCALE = float(2**18)
SCALE = 4096.0


def split(x):
    high = x.astype(jnp.bfloat16)
    return high, (x - high.astype(jnp.float32)).astype(jnp.bfloat16)


def turn(re, im, eighths):
    eighths %= 8
    if eighths % 2:
        re, im = (re + im) * HALF, (im - re) * HALF
        eighths -= 1
    return ((re, im), (im, -re), (-re, -im), (-im, re))[eighths // 2]


def pack_kernel(lesser_hbm, greater_hbm, coulomb_hbm, out_ref, lesser_ref, greater_ref, coulomb_ref, sems):
    copies = [
        pltpu.make_async_copy(source, target, sems.at[i])
        for i, (source, target) in enumerate(
            ((lesser_hbm, lesser_ref), (greater_hbm, greater_ref), (coulomb_hbm, coulomb_ref))
        )
    ]
    for copy in copies:
        copy.start()
    here = out_ref.shape[1] // 5
    stride = lesser_ref.shape[0] // here
    blocks = stride // 2
    out_ref[blocks:, :4 * here, :] = jnp.zeros_like(out_ref[blocks:, :4 * here, :])
    for which, ref in enumerate((lesser_ref, greater_ref)):
        copies[which].wait()
        for block in range(blocks):
            for part in range(2):
                at = (which * 2 + part) * here
                out_ref[block, at:at + here, :] = ref[pl.ds(block * 2 + part, here, stride=stride), :] * SCALE
    copies[2].wait()
    block = coulomb_ref[...]
    rows, wide = block.shape
    row = lax.broadcasted_iota(jnp.int32, (rows, LANES), 0)
    lane = lax.broadcasted_iota(jnp.int32, (rows, LANES), 1)
    total = None
    for group in range(wide // here):
        place = jnp.where(lane == row + group * rows, COULOMB_SCALE, 0.0).astype(jnp.bfloat16)
        turned = lax.dot_general(block, place, (((0,), (0,)), ((), ())), preferred_element_type=jnp.float32)
        turned = turned[group * here:(group + 1) * here, :]
        total = turned if total is None else total + turned
    for owner in range(out_ref.shape[0]):
        out_ref[owner, 4 * here:, :] = total


def unpack_kernel(x_ref, out_ref):
    sources, rows, _ = x_ref.shape
    extra = rows // 5
    width = out_ref.shape[1] // sources
    for group in range(out_ref.shape[0] // extra):
        pieces = [
            x_ref[source, 4 * extra:, group * width:(group + 1) * width] for source in range(sources)
        ]
        row = jnp.concatenate(pieces, axis=1) * (1.0 / COULOMB_SCALE)
        out_ref[group * extra:(group + 1) * extra, :] = row.astype(jnp.bfloat16)


def correlate_kernel(x_ref, matrices_ref, twiddle_ref, out_ref, total_ref, spread_ref):
    sources, here, lanes = x_ref.shape[0], x_ref.shape[1] // 5, x_ref.shape[2]
    rows = matrices_ref.shape[1]
    points = rows // 2
    pieces = sources * here // points
    per_piece = sources // pieces
    matrices = matrices_ref[...]

    def dft(re, im):
        x = jnp.concatenate([re, im], axis=0)
        x_high, x_low = split(x)
        both = jnp.dot(matrices, x_high, preferred_element_type=jnp.float32)
        return both[:rows] + both[rows:] + jnp.dot(matrices[:rows], x_low, preferred_element_type=jnp.float32)

    def piece(which, part, j):
        at = (which * 2 + part) * here
        return x_ref[j * per_piece:(j + 1) * per_piece, at:at + here, :].reshape(points, lanes)

    for r in range(RADIX // 2):
        for other in (r, r + RADIX // 2):
            spread_ref[2 * other] = jnp.broadcast_to(twiddle_ref[:, 2 * other:2 * other + 1], (points, lanes))
            spread_ref[2 * other + 1] = jnp.broadcast_to(twiddle_ref[:, 2 * other + 1:2 * other + 2], (points, lanes))
        sums = []
        for which in range(2):
            terms = []
            for j in range(4):
                re, im = piece(which, 0, j), piece(which, 1, j)
                if which:
                    im = -im
                terms.append(turn(re, im, r * j))
            even = [terms[0][k] + terms[2][k] for k in range(2)]
            odd = [terms[1][k] + terms[3][k] for k in range(2)]
            sums.append(([even[k] + odd[k] for k in range(2)], [even[k] - odd[k] for k in range(2)]))
        mixed = []
        for half, other in enumerate((r, r + RADIX // 2)):
            w_re, w_im = spread_ref[2 * other], spread_ref[2 * other + 1]
            turned = []
            for which in range(2):
                re, im = sums[which][half]
                turned.append((re * w_re - im * w_im, re * w_im + im * w_re))
            y = dft(
                jnp.concatenate([turned[0][0], turned[1][0]], axis=1),
                jnp.concatenate([turned[0][1], turned[1][1]], axis=1),
            )
            l_re, l_im = y[:points, :lanes], y[points:, :lanes]
            g_re, g_im = y[:points, lanes:], y[points:, lanes:]
            mixed.append((l_re * g_re + l_im * g_im, l_re * g_im - l_im * g_re))
        z = dft(
            jnp.concatenate([mixed[0][0], mixed[1][0]], axis=1),
            jnp.concatenate([mixed[0][1], mixed[1][1]], axis=1),
        )
        back = []
        for half, other in enumerate((r, r + RADIX // 2)):
            w_re, w_im = spread_ref[2 * other], spread_ref[2 * other + 1]
            re, im = z[:points, half * lanes:(half + 1) * lanes], z[points:, half * lanes:(half + 1) * lanes]
            back.append((re * w_re - im * w_im, re * w_im + im * w_re))
        both = [back[0][k] + back[1][k] for k in range(2)]
        apart = [back[0][k] - back[1][k] for k in range(2)]
        for j in range(4):
            re, im = turn(*(apart if j % 2 else both), r * j)
            if r == 0:
                total_ref[j, 0] = re
                total_ref[j, 1] = im
            else:
                total_ref[j, 0] += re
                total_ref[j, 1] += im
    energies = sources * here
    factor = -1.0 / (math.sqrt(energies) * 2 * energies * SCALE * SCALE)
    for j in range(pieces):
        for part in range(2):
            value = (total_ref[j, 1 - part] * factor).astype(jnp.bfloat16)
            out_ref[j * per_piece:(j + 1) * per_piece, part * here:(part + 1) * here, :] = value.reshape(
                per_piece, here, lanes
            )


def lies(owner, owners):
    return owner % APART * (owners // APART) + owner // APART


def screen_kernel(place_ref, polar_ref, *refs):
    *run_refs, out_ref, coulomb_ref = refs
    run, wide, order = run_refs[0].shape
    across = len(run_refs) // CORES
    groups = order // LANES
    here = polar_ref.shape[1] // 2
    stride = out_ref.shape[0] // here
    columns = stride // 2 // groups
    z, x, core = place_ref[0], place_ref[1], place_ref[2]
    for at, hop_x in enumerate(HOPS):
        for hop in range(run):
            chip = lax.rem(z + hop, run) * across + lax.rem(x + hop_x, across)
            coulomb_ref[chip * CORES + core] = run_refs[at][hop]
            coulomb_ref[chip * CORES + 1 - core] = run_refs[across + at][hop]
    rows = [
        jnp.concatenate([polar_ref[lies(c * groups + k, polar_ref.shape[0])] for k in range(groups)], axis=1)
        for c in range(columns)
    ]
    product = lax.dot_general(
        jnp.concatenate(rows, axis=0),
        coulomb_ref[...].reshape(order, order),
        (((1,), (1,)), ((), ())),
        preferred_element_type=jnp.float32,
    )
    for c in range(columns):
        for part in range(2):
            at = (c * 2 + part) * here
            for k in range(groups):
                out_ref[pl.ds((c * groups + k) * 2 + part, here, stride=stride), :] = product[
                    at:at + here, k * LANES:(k + 1) * LANES
                ]


def tables(energies):
    points = energies * 2 // RADIX
    angle = np.outer(np.arange(points), np.arange(points)) % points * (2 * np.pi / points)
    cos, sin = np.cos(angle), np.sin(angle)
    whole = np.block([[cos, sin], [-sin, cos]])
    high = whole.astype(jnp.bfloat16)
    low = (whole - high.astype(np.float64)).astype(jnp.bfloat16)
    twiddle = np.zeros((points, LANES), np.float32)
    for r in range(RADIX):
        turned = np.arange(points) * r * (np.pi / energies)
        twiddle[:, 2 * r], twiddle[:, 2 * r + 1] = np.cos(turned), -np.sin(turned)
    return np.concatenate([high, low]), twiddle


def rows_view(x):
    energies, _, columns, order = x.shape
    x = x.reshape(energies, 2, columns, order // LANES, LANES).transpose(0, 2, 3, 1, 4)
    x = with_layout_constraint(x, Layout(tuple(range(x.ndim))))
    return x.reshape(-1, LANES)


def pack(lesser, greater, coulomb, owners):
    here = lesser.shape[0]
    lesser, greater = rows_view(lesser), rows_view(greater)
    return pl.pallas_call(
        pack_kernel,
        out_shape=jax.ShapeDtypeStruct((owners, 5 * here, LANES), jnp.float32),
        in_specs=[pl.BlockSpec(memory_space=pltpu.HBM)] * 3,
        out_specs=pl.BlockSpec(memory_space=pltpu.VMEM),
        scratch_shapes=[pltpu.VMEM(x.shape, x.dtype) for x in (lesser, greater, coulomb)]
        + [pltpu.SemaphoreType.DMA((3,))],
        compiler_params=pltpu.CompilerParams(vmem_limit_bytes=16 << 20),
        name="pack",
    )(*(pltpu.with_memory_space_constraint(x, pltpu.HBM) for x in (lesser, greater, coulomb)))


def unpack(x, wide, order):
    return pl.pallas_call(
        unpack_kernel,
        out_shape=jax.ShapeDtypeStruct((wide, order), jnp.bfloat16),
        compiler_params=pltpu.CompilerParams(vmem_limit_bytes=16 << 20),
        name="unpack",
    )(x)


def correlate(x):
    owners, here, lanes = x.shape[0], x.shape[1] // 5, x.shape[2]
    energies = owners * here
    points = energies * 2 // RADIX
    matrices, twiddle = tables(energies)
    return pl.pallas_call(
        correlate_kernel,
        out_shape=jax.ShapeDtypeStruct((owners, 2 * here, lanes), jnp.bfloat16),
        scratch_shapes=[
            pltpu.VMEM((4, 2, points, lanes), jnp.float32),
            pltpu.VMEM((2 * RADIX, points, lanes), jnp.float32),
        ],
        compiler_params=pltpu.CompilerParams(vmem_limit_bytes=24 << 20),
        cost_estimate=pl.CostEstimate(
            flops=RADIX * 3 * 2 * (2 * points) ** 2 * 3 * lanes, bytes_accessed=x.size * 4 + x.size, transcendentals=0
        ),
        name="correlate",
    )(x, jnp.asarray(matrices), jnp.asarray(twiddle))


def screen(polar, runs, place, shape):
    energies, _, columns, order = shape
    run, wide, _ = runs[0].shape
    out = pl.pallas_call(
        screen_kernel,
        out_shape=jax.ShapeDtypeStruct((energies * columns * order * 2 // LANES, LANES), jnp.float32),
        in_specs=[pl.BlockSpec(memory_space=pltpu.SMEM)]
        + [pl.BlockSpec(memory_space=pltpu.VMEM)] * (1 + len(runs)),
        out_specs=pl.BlockSpec(memory_space=pltpu.VMEM),
        scratch_shapes=[pltpu.VMEM((len(runs) * run, wide, order), jnp.bfloat16)],
        compiler_params=pltpu.CompilerParams(vmem_limit_bytes=24 << 20),
        name="screen",
    )(place, polar, *runs)
    out = out.reshape(energies, columns, order // LANES, 2, LANES).transpose(0, 1, 3, 2, 4)
    return out.reshape(energies, columns, 2, order).transpose(0, 2, 1, 3)


def moved(x, sharers, hops):
    def source(at):
        z, x, core = at // (ACROSS * CORES), at // CORES % ACROSS, at % CORES
        z, x, core = (z + hops[0]) % RUN, (x + hops[1]) % ACROSS, (core + hops[2]) % CORES
        return (z * ACROSS + x) * CORES + core

    return lax.ppermute(x, "col", [(source(at), at) for at in range(sharers)])


def same_z(owners):
    return [[y * APART + z for y in range(owners // APART)] for z in range(APART)]


def same_y(owners):
    return [[y * APART + z for z in range(APART)] for y in range(owners // APART)]


def per_device(lesser, greater_transposed, coulomb):
    owners = lax.axis_size("energy")
    sharers = lax.axis_size("col")
    order = lesser.shape[3]
    packed = pack(lesser, greater_transposed, coulomb, owners)
    got = lax.all_to_all(packed.astype(jnp.float16), "energy", split_axis=0, concat_axis=0, tiled=True)
    got = got.astype(jnp.float32)
    wide = coulomb.shape[1]
    mine = unpack(got, wide, order)
    run = jnp.stack([mine] + [moved(mine, sharers, (hop, 0, 0)) for hop in range(1, RUN)])
    polar = correlate(got)
    run, polar = lax.optimization_barrier((run, polar))
    runs = [run] + [moved(run, sharers, (0, hop, 0)) for hop in HOPS[1:]]
    runs += [moved(run, sharers, (0, 0, 1)) for run in runs]
    polar = lax.all_to_all(polar, "energy", split_axis=0, concat_axis=0, axis_index_groups=same_z(owners), tiled=True)
    polar = polar.reshape((owners // APART, APART) + polar.shape[1:]).swapaxes(0, 1).reshape(polar.shape)
    polar = lax.all_to_all(polar, "energy", split_axis=0, concat_axis=0, axis_index_groups=same_y(owners), tiled=True)
    at = lax.axis_index("col")
    place = [lax.div(at, ACROSS * CORES), lax.rem(lax.div(at, CORES), ACROSS), lax.rem(at, CORES)]
    return screen(polar, runs, jnp.stack(place).astype(jnp.int32), lesser.shape)


def solution(mesh):
    placed = (P("energy", None, "col", None), P("energy", None, "col", None), P("energy", "col"))
    return jax.shard_map(
        per_device,
        mesh=mesh,
        in_specs=placed,
        out_specs=P("energy", None, "col", None),
        check_vma=False,
    )
```

```python
import functools
import math

import jax
import jax.numpy as jnp
import numpy as np
from jax import lax
from jax.experimental import pallas as pl
from jax.experimental.layout import Layout, with_layout_constraint
from jax.experimental.pallas import tpu as pltpu
from jax.sharding import PartitionSpec as P

LANES = 128
RADIX = 8
RUN, ACROSS, CORES = 3, 4, 2
HOPS = (0, 1, 3, 2)
HALF = math.sqrt(0.5)
COULOMB_SCALE = float(2**18)
SCALE = 4096.0


def split(x):
    high = x.astype(jnp.bfloat16)
    return high, (x - high.astype(jnp.float32)).astype(jnp.bfloat16)


def turn(re, im, eighths):
    eighths %= 8
    if eighths % 2:
        re, im = (re + im) * HALF, (im - re) * HALF
        eighths -= 1
    return ((re, im), (im, -re), (-re, -im), (-im, re))[eighths // 2]


def pack_kernel(lesser_hbm, greater_hbm, coulomb_hbm, out_ref, lesser_ref, greater_ref, coulomb_ref, sems):
    copies = [
        pltpu.make_async_copy(source, target, sems.at[i])
        for i, (source, target) in enumerate(
            ((lesser_hbm, lesser_ref), (greater_hbm, greater_ref), (coulomb_hbm, coulomb_ref))
        )
    ]
    for copy in copies:
        copy.start()
    here = out_ref.shape[1] // 5
    stride = lesser_ref.shape[0] // here
    blocks = stride // 2
    out_ref[blocks:, :4 * here, :] = jnp.zeros_like(out_ref[blocks:, :4 * here, :])
    for which, ref in enumerate((lesser_ref, greater_ref)):
        copies[which].wait()
        for block in range(blocks):
            for part in range(2):
                at = (which * 2 + part) * here
                out_ref[block, at:at + here, :] = ref[pl.ds(block * 2 + part, here, stride=stride), :] * SCALE
    copies[2].wait()
    block = coulomb_ref[...]
    rows, wide = block.shape
    row = lax.broadcasted_iota(jnp.int32, (rows, LANES), 0)
    lane = lax.broadcasted_iota(jnp.int32, (rows, LANES), 1)
    total = None
    for group in range(wide // here):
        place = jnp.where(lane == row + group * rows, COULOMB_SCALE, 0.0).astype(jnp.bfloat16)
        turned = lax.dot_general(block, place, (((0,), (0,)), ((), ())), preferred_element_type=jnp.float32)
        turned = turned[group * here:(group + 1) * here, :]
        total = turned if total is None else total + turned
    for owner in range(out_ref.shape[0]):
        out_ref[owner, 4 * here:, :] = total


def unpack_kernel(x_ref, out_ref):
    sources, rows, _ = x_ref.shape
    extra = rows // 5
    width = out_ref.shape[1] // sources
    for group in range(out_ref.shape[0] // extra):
        pieces = [
            x_ref[source, 4 * extra:, group * width:(group + 1) * width] for source in range(sources)
        ]
        row = jnp.concatenate(pieces, axis=1) * (1.0 / COULOMB_SCALE)
        out_ref[group * extra:(group + 1) * extra, :] = row.astype(jnp.bfloat16)


def correlate_kernel(x_ref, matrices_ref, twiddle_ref, out_ref, total_ref, spread_ref):
    sources, here, lanes = x_ref.shape[0], x_ref.shape[1] // 5, x_ref.shape[2]
    rows = matrices_ref.shape[1]
    points = rows // 2
    pieces = sources * here // points
    per_piece = sources // pieces
    matrices = matrices_ref[...]

    def dft(re, im):
        x = jnp.concatenate([re, im], axis=0)
        x_high, x_low = split(x)
        both = jnp.dot(matrices, x_high, preferred_element_type=jnp.float32)
        return both[:rows] + both[rows:] + jnp.dot(matrices[:rows], x_low, preferred_element_type=jnp.float32)

    def piece(which, part, j):
        at = (which * 2 + part) * here
        return x_ref[j * per_piece:(j + 1) * per_piece, at:at + here, :].reshape(points, lanes)

    for r in range(RADIX // 2):
        for other in (r, r + RADIX // 2):
            spread_ref[2 * other] = jnp.broadcast_to(twiddle_ref[:, 2 * other:2 * other + 1], (points, lanes))
            spread_ref[2 * other + 1] = jnp.broadcast_to(twiddle_ref[:, 2 * other + 1:2 * other + 2], (points, lanes))
        sums = []
        for which in range(2):
            terms = []
            for j in range(4):
                re, im = piece(which, 0, j), piece(which, 1, j)
                if which:
                    im = -im
                terms.append(turn(re, im, r * j))
            even = [terms[0][k] + terms[2][k] for k in range(2)]
            odd = [terms[1][k] + terms[3][k] for k in range(2)]
            sums.append(([even[k] + odd[k] for k in range(2)], [even[k] - odd[k] for k in range(2)]))
        mixed = []
        for half, other in enumerate((r, r + RADIX // 2)):
            w_re, w_im = spread_ref[2 * other], spread_ref[2 * other + 1]
            turned = []
            for which in range(2):
                re, im = sums[which][half]
                turned.append((re * w_re - im * w_im, re * w_im + im * w_re))
            y = dft(
                jnp.concatenate([turned[0][0], turned[1][0]], axis=1),
                jnp.concatenate([turned[0][1], turned[1][1]], axis=1),
            )
            l_re, l_im = y[:points, :lanes], y[points:, :lanes]
            g_re, g_im = y[:points, lanes:], y[points:, lanes:]
            mixed.append((l_re * g_re + l_im * g_im, l_re * g_im - l_im * g_re))
        z = dft(
            jnp.concatenate([mixed[0][0], mixed[1][0]], axis=1),
            jnp.concatenate([mixed[0][1], mixed[1][1]], axis=1),
        )
        back = []
        for half, other in enumerate((r, r + RADIX // 2)):
            w_re, w_im = spread_ref[2 * other], spread_ref[2 * other + 1]
            re, im = z[:points, half * lanes:(half + 1) * lanes], z[points:, half * lanes:(half + 1) * lanes]
            back.append((re * w_re - im * w_im, re * w_im + im * w_re))
        both = [back[0][k] + back[1][k] for k in range(2)]
        apart = [back[0][k] - back[1][k] for k in range(2)]
        for j in range(4):
            re, im = turn(*(apart if j % 2 else both), r * j)
            if r == 0:
                total_ref[j, 0] = re
                total_ref[j, 1] = im
            else:
                total_ref[j, 0] += re
                total_ref[j, 1] += im
    energies = sources * here
    factor = -1.0 / (math.sqrt(energies) * 2 * energies * SCALE * SCALE)
    for j in range(pieces):
        for part in range(2):
            value = (total_ref[j, 1 - part] * factor).astype(jnp.bfloat16)
            out_ref[j * per_piece:(j + 1) * per_piece, part * here:(part + 1) * here, :] = value.reshape(
                per_piece, here, lanes
            )


def screen_kernel(place_ref, polar_ref, *refs):
    *run_refs, out_ref, coulomb_ref = refs
    run, wide, order = run_refs[0].shape
    across = len(run_refs) // CORES
    groups = order // LANES
    here = polar_ref.shape[1] // 2
    stride = out_ref.shape[0] // here
    columns = stride // 2 // groups
    z, x, core = place_ref[0], place_ref[1], place_ref[2]
    for at, hop_x in enumerate(HOPS):
        for hop in range(run):
            chip = lax.rem(z + hop, run) * across + lax.rem(x + hop_x, across)
            coulomb_ref[chip * CORES + core] = run_refs[at][hop]
            coulomb_ref[chip * CORES + 1 - core] = run_refs[across + at][hop]
    rows = [
        jnp.concatenate([polar_ref[c * groups + k] for k in range(groups)], axis=1) for c in range(columns)
    ]
    product = lax.dot_general(
        jnp.concatenate(rows, axis=0),
        coulomb_ref[...].reshape(order, order),
        (((1,), (1,)), ((), ())),
        preferred_element_type=jnp.float32,
    )
    for c in range(columns):
        for part in range(2):
            at = (c * 2 + part) * here
            for k in range(groups):
                out_ref[pl.ds((c * groups + k) * 2 + part, here, stride=stride), :] = product[
                    at:at + here, k * LANES:(k + 1) * LANES
                ]


def tables(energies):
    points = energies * 2 // RADIX
    angle = np.outer(np.arange(points), np.arange(points)) % points * (2 * np.pi / points)
    cos, sin = np.cos(angle), np.sin(angle)
    whole = np.block([[cos, sin], [-sin, cos]])
    high = whole.astype(jnp.bfloat16)
    low = (whole - high.astype(np.float64)).astype(jnp.bfloat16)
    twiddle = np.zeros((points, LANES), np.float32)
    for r in range(RADIX):
        turned = np.arange(points) * r * (np.pi / energies)
        twiddle[:, 2 * r], twiddle[:, 2 * r + 1] = np.cos(turned), -np.sin(turned)
    return np.concatenate([high, low]), twiddle


def rows_view(x):
    energies, _, columns, order = x.shape
    x = x.reshape(energies, 2, columns, order // LANES, LANES).transpose(0, 2, 3, 1, 4)
    x = with_layout_constraint(x, Layout(tuple(range(x.ndim))))
    return x.reshape(-1, LANES)


def pack(lesser, greater, coulomb, owners):
    here = lesser.shape[0]
    lesser, greater = rows_view(lesser), rows_view(greater)
    return pl.pallas_call(
        pack_kernel,
        out_shape=jax.ShapeDtypeStruct((owners, 5 * here, LANES), jnp.float32),
        in_specs=[pl.BlockSpec(memory_space=pltpu.HBM)] * 3,
        out_specs=pl.BlockSpec(memory_space=pltpu.VMEM),
        scratch_shapes=[pltpu.VMEM(x.shape, x.dtype) for x in (lesser, greater, coulomb)]
        + [pltpu.SemaphoreType.DMA((3,))],
        compiler_params=pltpu.CompilerParams(vmem_limit_bytes=16 << 20),
        name="pack",
    )(*(pltpu.with_memory_space_constraint(x, pltpu.HBM) for x in (lesser, greater, coulomb)))


def unpack(x, wide, order):
    return pl.pallas_call(
        unpack_kernel,
        out_shape=jax.ShapeDtypeStruct((wide, order), jnp.bfloat16),
        compiler_params=pltpu.CompilerParams(vmem_limit_bytes=16 << 20),
        name="unpack",
    )(x)


def correlate(x):
    owners, here, lanes = x.shape[0], x.shape[1] // 5, x.shape[2]
    energies = owners * here
    points = energies * 2 // RADIX
    matrices, twiddle = tables(energies)
    return pl.pallas_call(
        correlate_kernel,
        out_shape=jax.ShapeDtypeStruct((owners, 2 * here, lanes), jnp.bfloat16),
        scratch_shapes=[
            pltpu.VMEM((4, 2, points, lanes), jnp.float32),
            pltpu.VMEM((2 * RADIX, points, lanes), jnp.float32),
        ],
        compiler_params=pltpu.CompilerParams(vmem_limit_bytes=24 << 20),
        cost_estimate=pl.CostEstimate(
            flops=RADIX * 3 * 2 * (2 * points) ** 2 * 3 * lanes, bytes_accessed=x.size * 4 + x.size, transcendentals=0
        ),
        name="correlate",
    )(x, jnp.asarray(matrices), jnp.asarray(twiddle))


def screen(polar, runs, place, shape):
    energies, _, columns, order = shape
    run, wide, _ = runs[0].shape
    out = pl.pallas_call(
        screen_kernel,
        out_shape=jax.ShapeDtypeStruct((energies * columns * order * 2 // LANES, LANES), jnp.float32),
        in_specs=[pl.BlockSpec(memory_space=pltpu.SMEM)]
        + [pl.BlockSpec(memory_space=pltpu.VMEM)] * (1 + len(runs)),
        out_specs=pl.BlockSpec(memory_space=pltpu.VMEM),
        scratch_shapes=[pltpu.VMEM((len(runs) * run, wide, order), jnp.bfloat16)],
        compiler_params=pltpu.CompilerParams(vmem_limit_bytes=24 << 20),
        name="screen",
    )(place, polar, *runs)
    out = out.reshape(energies, columns, order // LANES, 2, LANES).transpose(0, 1, 3, 2, 4)
    return out.reshape(energies, columns, 2, order).transpose(0, 2, 1, 3)


def moved(x, sharers, hops):
    def source(at):
        z, x, core = at // (ACROSS * CORES), at // CORES % ACROSS, at % CORES
        z, x, core = (z + hops[0]) % RUN, (x + hops[1]) % ACROSS, (core + hops[2]) % CORES
        return (z * ACROSS + x) * CORES + core

    return lax.ppermute(x, "col", [(source(at), at) for at in range(sharers)])


def per_device(lesser, greater_transposed, coulomb):
    owners = lax.axis_size("energy")
    sharers = lax.axis_size("col")
    order = lesser.shape[3]
    packed = pack(lesser, greater_transposed, coulomb, owners)
    got = lax.all_to_all(packed.astype(jnp.float16), "energy", split_axis=0, concat_axis=0, tiled=True)
    got = got.astype(jnp.float32)
    wide = coulomb.shape[1]
    mine = unpack(got, wide, order)
    run = jnp.stack([mine] + [moved(mine, sharers, (hop, 0, 0)) for hop in range(1, RUN)])
    polar = correlate(got)
    run, polar = lax.optimization_barrier((run, polar))
    ahead, behind = moved(run, sharers, (0, 1, 0)), moved(run, sharers, (0, ACROSS - 1, 0))
    runs = [run, ahead, behind, moved(ahead, sharers, (0, 1, 0))]
    runs += [moved(run, sharers, (0, 0, 1)) for run in runs]
    polar = lax.all_to_all(polar, "energy", split_axis=0, concat_axis=0, tiled=True)
    at = lax.axis_index("col")
    place = [lax.div(at, ACROSS * CORES), lax.rem(lax.div(at, CORES), ACROSS), lax.rem(at, CORES)]
    return screen(polar, runs, jnp.stack(place).astype(jnp.int32), lesser.shape)


def solution(mesh):
    placed = (P("energy", None, "col", None), P("energy", None, "col", None), P("energy", "col"))
    return jax.shard_map(
        per_device,
        mesh=mesh,
        in_specs=placed,
        out_specs=P("energy", None, "col", None),
        check_vma=False,
    )
```

```python
import functools
import math

import jax
import jax.numpy as jnp
import numpy as np
from jax import lax
from jax.experimental import pallas as pl
from jax.experimental.layout import Layout, with_layout_constraint
from jax.experimental.pallas import tpu as pltpu
from jax.sharding import PartitionSpec as P

LANES = 128
RADIX = 8
RUN, ACROSS, CORES = 3, 4, 2
HOPS = (0, 1, 3, 2)
HALF = math.sqrt(0.5)
COULOMB_SCALE = float(2**18)
SCALE = 4096.0


def split(x):
    high = x.astype(jnp.bfloat16)
    return high, (x - high.astype(jnp.float32)).astype(jnp.bfloat16)


def turn(re, im, eighths):
    eighths %= 8
    if eighths % 2:
        re, im = (re + im) * HALF, (im - re) * HALF
        eighths -= 1
    return ((re, im), (im, -re), (-re, -im), (-im, re))[eighths // 2]


def pack_kernel(lesser_hbm, greater_hbm, coulomb_hbm, out_ref, lesser_ref, greater_ref, coulomb_ref, sems):
    copies = [
        pltpu.make_async_copy(source, target, sems.at[i])
        for i, (source, target) in enumerate(
            ((lesser_hbm, lesser_ref), (greater_hbm, greater_ref), (coulomb_hbm, coulomb_ref))
        )
    ]
    for copy in copies:
        copy.start()
    here = out_ref.shape[1] // 5
    stride = lesser_ref.shape[0] // here
    blocks = stride // 2
    out_ref[blocks:, :4 * here, :] = jnp.zeros_like(out_ref[blocks:, :4 * here, :])
    for which, ref in enumerate((lesser_ref, greater_ref)):
        copies[which].wait()
        for block in range(blocks):
            for part in range(2):
                at = (which * 2 + part) * here
                out_ref[block, at:at + here, :] = ref[pl.ds(block * 2 + part, here, stride=stride), :] * SCALE
    copies[2].wait()
    block = coulomb_ref[...]
    rows, wide = block.shape
    row = lax.broadcasted_iota(jnp.int32, (rows, LANES), 0)
    lane = lax.broadcasted_iota(jnp.int32, (rows, LANES), 1)
    total = None
    for group in range(wide // here):
        place = jnp.where(lane == row + group * rows, COULOMB_SCALE, 0.0).astype(jnp.bfloat16)
        turned = lax.dot_general(block, place, (((0,), (0,)), ((), ())), preferred_element_type=jnp.float32)
        turned = turned[group * here:(group + 1) * here, :]
        total = turned if total is None else total + turned
    for owner in range(out_ref.shape[0]):
        out_ref[owner, 4 * here:, :] = total


def unpack_kernel(x_ref, out_ref):
    sources, rows, _ = x_ref.shape
    extra = rows // 5
    width = out_ref.shape[1] // sources
    for group in range(out_ref.shape[0] // extra):
        pieces = [
            x_ref[source, 4 * extra:, group * width:(group + 1) * width] for source in range(sources)
        ]
        row = jnp.concatenate(pieces, axis=1) * (1.0 / COULOMB_SCALE)
        out_ref[group * extra:(group + 1) * extra, :] = row.astype(jnp.bfloat16)


def correlate_kernel(x_ref, matrices_ref, twiddle_ref, out_ref, total_ref, spread_ref):
    sources, here, lanes = x_ref.shape[0], x_ref.shape[1] // 5, x_ref.shape[2]
    rows = matrices_ref.shape[1]
    points = rows // 2
    pieces = sources * here // points
    per_piece = sources // pieces
    matrices = matrices_ref[...]

    def dft(re, im):
        x = jnp.concatenate([re, im], axis=0)
        x_high, x_low = split(x)
        both = jnp.dot(matrices, x_high, preferred_element_type=jnp.float32)
        return both[:rows] + both[rows:] + jnp.dot(matrices[:rows], x_low, preferred_element_type=jnp.float32)

    def piece(which, part, j):
        at = (which * 2 + part) * here
        return x_ref[j * per_piece:(j + 1) * per_piece, at:at + here, :].reshape(points, lanes)

    for r in range(RADIX // 2):
        for other in (r, r + RADIX // 2):
            spread_ref[2 * other] = jnp.broadcast_to(twiddle_ref[:, 2 * other:2 * other + 1], (points, lanes))
            spread_ref[2 * other + 1] = jnp.broadcast_to(twiddle_ref[:, 2 * other + 1:2 * other + 2], (points, lanes))
        sums = []
        for which in range(2):
            terms = []
            for j in range(4):
                re, im = piece(which, 0, j), piece(which, 1, j)
                if which:
                    im = -im
                terms.append(turn(re, im, r * j))
            even = [terms[0][k] + terms[2][k] for k in range(2)]
            odd = [terms[1][k] + terms[3][k] for k in range(2)]
            sums.append(([even[k] + odd[k] for k in range(2)], [even[k] - odd[k] for k in range(2)]))
        mixed = []
        for half, other in enumerate((r, r + RADIX // 2)):
            w_re, w_im = spread_ref[2 * other], spread_ref[2 * other + 1]
            turned = []
            for which in range(2):
                re, im = sums[which][half]
                turned.append((re * w_re - im * w_im, re * w_im + im * w_re))
            y = dft(
                jnp.concatenate([turned[0][0], turned[1][0]], axis=1),
                jnp.concatenate([turned[0][1], turned[1][1]], axis=1),
            )
            l_re, l_im = y[:points, :lanes], y[points:, :lanes]
            g_re, g_im = y[:points, lanes:], y[points:, lanes:]
            mixed.append((l_re * g_re + l_im * g_im, l_re * g_im - l_im * g_re))
        z = dft(
            jnp.concatenate([mixed[0][0], mixed[1][0]], axis=1),
            jnp.concatenate([mixed[0][1], mixed[1][1]], axis=1),
        )
        back = []
        for half, other in enumerate((r, r + RADIX // 2)):
            w_re, w_im = spread_ref[2 * other], spread_ref[2 * other + 1]
            re, im = z[:points, half * lanes:(half + 1) * lanes], z[points:, half * lanes:(half + 1) * lanes]
            back.append((re * w_re - im * w_im, re * w_im + im * w_re))
        both = [back[0][k] + back[1][k] for k in range(2)]
        apart = [back[0][k] - back[1][k] for k in range(2)]
        for j in range(4):
            re, im = turn(*(apart if j % 2 else both), r * j)
            if r == 0:
                total_ref[j, 0] = re
                total_ref[j, 1] = im
            else:
                total_ref[j, 0] += re
                total_ref[j, 1] += im
    energies = sources * here
    factor = -1.0 / (math.sqrt(energies) * 2 * energies * SCALE * SCALE)
    for j in range(pieces):
        for part in range(2):
            value = (total_ref[j, 1 - part] * factor).astype(jnp.bfloat16)
            out_ref[j * per_piece:(j + 1) * per_piece, part * here:(part + 1) * here, :] = value.reshape(
                per_piece, here, lanes
            )


def screen_kernel(place_ref, polar_ref, *refs):
    *run_refs, out_ref, coulomb_ref = refs
    run, wide, order = run_refs[0].shape
    across = len(run_refs) // CORES
    groups = order // LANES
    here = polar_ref.shape[1] // 2
    stride = out_ref.shape[0] // here
    columns = stride // 2 // groups
    z, x, core = place_ref[0], place_ref[1], place_ref[2]
    for at, hop_x in enumerate(HOPS):
        for hop in range(run):
            chip = lax.rem(z + hop, run) * across + lax.rem(x + hop_x, across)
            coulomb_ref[chip * CORES + core] = run_refs[at][hop]
            coulomb_ref[chip * CORES + 1 - core] = run_refs[across + at][hop]
    rows = [
        jnp.concatenate([polar_ref[c * groups + k] for k in range(groups)], axis=1) for c in range(columns)
    ]
    product = lax.dot_general(
        jnp.concatenate(rows, axis=0),
        coulomb_ref[...].reshape(order, order),
        (((1,), (1,)), ((), ())),
        preferred_element_type=jnp.float32,
    )
    for c in range(columns):
        for part in range(2):
            at = (c * 2 + part) * here
            for k in range(groups):
                out_ref[pl.ds((c * groups + k) * 2 + part, here, stride=stride), :] = product[
                    at:at + here, k * LANES:(k + 1) * LANES
                ]


def tables(energies):
    points = energies * 2 // RADIX
    angle = np.outer(np.arange(points), np.arange(points)) % points * (2 * np.pi / points)
    cos, sin = np.cos(angle), np.sin(angle)
    whole = np.block([[cos, sin], [-sin, cos]])
    high = whole.astype(jnp.bfloat16)
    low = (whole - high.astype(np.float64)).astype(jnp.bfloat16)
    twiddle = np.zeros((points, LANES), np.float32)
    for r in range(RADIX):
        turned = np.arange(points) * r * (np.pi / energies)
        twiddle[:, 2 * r], twiddle[:, 2 * r + 1] = np.cos(turned), -np.sin(turned)
    return np.concatenate([high, low]), twiddle


def rows_view(x):
    energies, _, columns, order = x.shape
    x = x.reshape(energies, 2, columns, order // LANES, LANES).transpose(0, 2, 3, 1, 4)
    x = with_layout_constraint(x, Layout(tuple(range(x.ndim))))
    return x.reshape(-1, LANES)


def pack(lesser, greater, coulomb, owners):
    here = lesser.shape[0]
    lesser, greater = rows_view(lesser), rows_view(greater)
    return pl.pallas_call(
        pack_kernel,
        out_shape=jax.ShapeDtypeStruct((owners, 5 * here, LANES), jnp.float32),
        in_specs=[pl.BlockSpec(memory_space=pltpu.HBM)] * 3,
        out_specs=pl.BlockSpec(memory_space=pltpu.VMEM),
        scratch_shapes=[pltpu.VMEM(x.shape, x.dtype) for x in (lesser, greater, coulomb)]
        + [pltpu.SemaphoreType.DMA((3,))],
        compiler_params=pltpu.CompilerParams(vmem_limit_bytes=16 << 20),
        name="pack",
    )(*(pltpu.with_memory_space_constraint(x, pltpu.HBM) for x in (lesser, greater, coulomb)))


def unpack(x, wide, order):
    return pl.pallas_call(
        unpack_kernel,
        out_shape=jax.ShapeDtypeStruct((wide, order), jnp.bfloat16),
        compiler_params=pltpu.CompilerParams(vmem_limit_bytes=16 << 20),
        name="unpack",
    )(x)


def correlate(x):
    owners, here, lanes = x.shape[0], x.shape[1] // 5, x.shape[2]
    energies = owners * here
    points = energies * 2 // RADIX
    matrices, twiddle = tables(energies)
    return pl.pallas_call(
        correlate_kernel,
        out_shape=jax.ShapeDtypeStruct((owners, 2 * here, lanes), jnp.bfloat16),
        scratch_shapes=[
            pltpu.VMEM((4, 2, points, lanes), jnp.float32),
            pltpu.VMEM((2 * RADIX, points, lanes), jnp.float32),
        ],
        compiler_params=pltpu.CompilerParams(vmem_limit_bytes=24 << 20),
        cost_estimate=pl.CostEstimate(
            flops=RADIX * 3 * 2 * (2 * points) ** 2 * 3 * lanes, bytes_accessed=x.size * 4 + x.size, transcendentals=0
        ),
        name="correlate",
    )(x, jnp.asarray(matrices), jnp.asarray(twiddle))


def screen(polar, runs, place, shape):
    energies, _, columns, order = shape
    run, wide, _ = runs[0].shape
    out = pl.pallas_call(
        screen_kernel,
        out_shape=jax.ShapeDtypeStruct((energies * columns * order * 2 // LANES, LANES), jnp.float32),
        in_specs=[pl.BlockSpec(memory_space=pltpu.SMEM)]
        + [pl.BlockSpec(memory_space=pltpu.VMEM)] * (1 + len(runs)),
        out_specs=pl.BlockSpec(memory_space=pltpu.VMEM),
        scratch_shapes=[pltpu.VMEM((len(runs) * run, wide, order), jnp.bfloat16)],
        compiler_params=pltpu.CompilerParams(vmem_limit_bytes=24 << 20),
        name="screen",
    )(place, polar, *runs)
    out = out.reshape(energies, columns, order // LANES, 2, LANES).transpose(0, 1, 3, 2, 4)
    return out.reshape(energies, columns, 2, order).transpose(0, 2, 1, 3)


def moved(x, sharers, hops):
    def source(at):
        z, x, core = at // (ACROSS * CORES), at // CORES % ACROSS, at % CORES
        z, x, core = (z + hops[0]) % RUN, (x + hops[1]) % ACROSS, (core + hops[2]) % CORES
        return (z * ACROSS + x) * CORES + core

    return lax.ppermute(x, "col", [(source(at), at) for at in range(sharers)])


def per_device(lesser, greater_transposed, coulomb):
    owners = lax.axis_size("energy")
    sharers = lax.axis_size("col")
    order = lesser.shape[3]
    packed = pack(lesser, greater_transposed, coulomb, owners)
    got = lax.all_to_all(packed.astype(jnp.float16), "energy", split_axis=0, concat_axis=0, tiled=True)
    got = got.astype(jnp.float32)
    wide = coulomb.shape[1]
    mine = unpack(got, wide, order)
    run = jnp.stack([mine] + [moved(mine, sharers, (hop, 0, 0)) for hop in range(1, RUN)])
    polar = correlate(got)
    ahead, behind = moved(run, sharers, (0, 1, 0)), moved(run, sharers, (0, ACROSS - 1, 0))
    runs = [run, ahead, behind, moved(ahead, sharers, (0, 1, 0))]
    runs += [moved(run, sharers, (0, 0, 1)) for run in runs]
    polar = lax.all_to_all(polar, "energy", split_axis=0, concat_axis=0, tiled=True)
    at = lax.axis_index("col")
    place = [lax.div(at, ACROSS * CORES), lax.rem(lax.div(at, CORES), ACROSS), lax.rem(at, CORES)]
    return screen(polar, runs, jnp.stack(place).astype(jnp.int32), lesser.shape)


def solution(mesh):
    placed = (P("energy", None, "col", None), P("energy", None, "col", None), P("energy", "col"))
    return jax.shard_map(
        per_device,
        mesh=mesh,
        in_specs=placed,
        out_specs=P("energy", None, "col", None),
        check_vma=False,
    )
```

```python
import functools
import math

import jax
import jax.numpy as jnp
import numpy as np
from jax import lax
from jax.experimental import pallas as pl
from jax.experimental.layout import Layout, with_layout_constraint
from jax.experimental.pallas import tpu as pltpu
from jax.sharding import PartitionSpec as P

LANES = 128
RADIX = 8
RUN, ACROSS, CORES = 3, 4, 2
HOPS = (0, 1, 3, 2)
HALF = math.sqrt(0.5)
COULOMB_SCALE = float(2**18)
SCALE = 4096.0


def split(x):
    high = x.astype(jnp.bfloat16)
    return high, (x - high.astype(jnp.float32)).astype(jnp.bfloat16)


def turn(re, im, eighths):
    eighths %= 8
    if eighths % 2:
        re, im = (re + im) * HALF, (im - re) * HALF
        eighths -= 1
    return ((re, im), (im, -re), (-re, -im), (-im, re))[eighths // 2]


def pack_kernel(lesser_hbm, greater_hbm, coulomb_hbm, out_ref, lesser_ref, greater_ref, coulomb_ref, sems):
    copies = [
        pltpu.make_async_copy(source, target, sems.at[i])
        for i, (source, target) in enumerate(
            ((lesser_hbm, lesser_ref), (greater_hbm, greater_ref), (coulomb_hbm, coulomb_ref))
        )
    ]
    for copy in copies:
        copy.start()
    here = out_ref.shape[1] // 5
    stride = lesser_ref.shape[0] // here
    blocks = stride // 2
    out_ref[blocks:, :4 * here, :] = jnp.zeros_like(out_ref[blocks:, :4 * here, :])
    for which, ref in enumerate((lesser_ref, greater_ref)):
        copies[which].wait()
        for block in range(blocks):
            for part in range(2):
                at = (which * 2 + part) * here
                out_ref[block, at:at + here, :] = ref[pl.ds(block * 2 + part, here, stride=stride), :] * SCALE
    copies[2].wait()
    block = coulomb_ref[...]
    rows, wide = block.shape
    row = lax.broadcasted_iota(jnp.int32, (rows, LANES), 0)
    lane = lax.broadcasted_iota(jnp.int32, (rows, LANES), 1)
    total = None
    for group in range(wide // here):
        place = jnp.where(lane == row + group * rows, COULOMB_SCALE, 0.0).astype(jnp.bfloat16)
        turned = lax.dot_general(block, place, (((0,), (0,)), ((), ())), preferred_element_type=jnp.float32)
        turned = turned[group * here:(group + 1) * here, :]
        total = turned if total is None else total + turned
    for owner in range(out_ref.shape[0]):
        out_ref[owner, 4 * here:, :] = total


def unpack_kernel(x_ref, out_ref):
    sources, rows, _ = x_ref.shape
    extra = rows // 5
    width = out_ref.shape[1] // sources
    for group in range(out_ref.shape[0] // extra):
        pieces = [
            x_ref[source, 4 * extra:, group * width:(group + 1) * width] for source in range(sources)
        ]
        row = jnp.concatenate(pieces, axis=1) * (1.0 / COULOMB_SCALE)
        out_ref[group * extra:(group + 1) * extra, :] = row.astype(jnp.bfloat16)


def correlate_kernel(x_ref, matrices_ref, twiddle_ref, out_ref, total_ref, spread_ref):
    sources, here, lanes = x_ref.shape[0], x_ref.shape[1] // 5, x_ref.shape[2]
    rows = matrices_ref.shape[1]
    points = rows // 2
    pieces = sources * here // points
    per_piece = sources // pieces
    matrices = matrices_ref[...]

    def dft(re, im):
        x = jnp.concatenate([re, im], axis=0)
        x_high, x_low = split(x)
        both = jnp.dot(matrices, x_high, preferred_element_type=jnp.float32)
        return both[:rows] + both[rows:] + jnp.dot(matrices[:rows], x_low, preferred_element_type=jnp.float32)

    def piece(which, part, j):
        at = (which * 2 + part) * here
        return x_ref[j * per_piece:(j + 1) * per_piece, at:at + here, :].reshape(points, lanes)

    for r in range(RADIX // 2):
        for other in (r, r + RADIX // 2):
            spread_ref[2 * other] = jnp.broadcast_to(twiddle_ref[:, 2 * other:2 * other + 1], (points, lanes))
            spread_ref[2 * other + 1] = jnp.broadcast_to(twiddle_ref[:, 2 * other + 1:2 * other + 2], (points, lanes))
        sums = []
        for which in range(2):
            terms = []
            for j in range(4):
                re, im = piece(which, 0, j), piece(which, 1, j)
                if which:
                    im = -im
                terms.append(turn(re, im, r * j))
            even = [terms[0][k] + terms[2][k] for k in range(2)]
            odd = [terms[1][k] + terms[3][k] for k in range(2)]
            sums.append(([even[k] + odd[k] for k in range(2)], [even[k] - odd[k] for k in range(2)]))
        mixed = []
        for half, other in enumerate((r, r + RADIX // 2)):
            w_re, w_im = spread_ref[2 * other], spread_ref[2 * other + 1]
            turned = []
            for which in range(2):
                re, im = sums[which][half]
                turned.append((re * w_re - im * w_im, re * w_im + im * w_re))
            y = dft(
                jnp.concatenate([turned[0][0], turned[1][0]], axis=1),
                jnp.concatenate([turned[0][1], turned[1][1]], axis=1),
            )
            l_re, l_im = y[:points, :lanes], y[points:, :lanes]
            g_re, g_im = y[:points, lanes:], y[points:, lanes:]
            mixed.append((l_re * g_re + l_im * g_im, l_re * g_im - l_im * g_re))
        z = dft(
            jnp.concatenate([mixed[0][0], mixed[1][0]], axis=1),
            jnp.concatenate([mixed[0][1], mixed[1][1]], axis=1),
        )
        back = []
        for half, other in enumerate((r, r + RADIX // 2)):
            w_re, w_im = spread_ref[2 * other], spread_ref[2 * other + 1]
            re, im = z[:points, half * lanes:(half + 1) * lanes], z[points:, half * lanes:(half + 1) * lanes]
            back.append((re * w_re - im * w_im, re * w_im + im * w_re))
        both = [back[0][k] + back[1][k] for k in range(2)]
        apart = [back[0][k] - back[1][k] for k in range(2)]
        for j in range(4):
            re, im = turn(*(apart if j % 2 else both), r * j)
            if r == 0:
                total_ref[j, 0] = re
                total_ref[j, 1] = im
            else:
                total_ref[j, 0] += re
                total_ref[j, 1] += im
    energies = sources * here
    factor = -1.0 / (math.sqrt(energies) * 2 * energies * SCALE * SCALE)
    for j in range(pieces):
        for part in range(2):
            value = (total_ref[j, 1 - part] * factor).astype(jnp.bfloat16)
            out_ref[j * per_piece:(j + 1) * per_piece, part * here:(part + 1) * here, :] = value.reshape(
                per_piece, here, lanes
            )


def screen_kernel(place_ref, polar_ref, *refs):
    *run_refs, out_ref, coulomb_ref = refs
    run, wide, order = run_refs[0].shape
    across = len(run_refs) // CORES
    groups = order // LANES
    here = polar_ref.shape[1] // 2
    stride = out_ref.shape[0] // here
    columns = stride // 2 // groups
    z, x, core = place_ref[0], place_ref[1], place_ref[2]
    for at, hop_x in enumerate(HOPS):
        for hop in range(run):
            chip = lax.rem(z + hop, run) * across + lax.rem(x + hop_x, across)
            coulomb_ref[chip * CORES + core] = run_refs[at][hop]
            coulomb_ref[chip * CORES + 1 - core] = run_refs[across + at][hop]
    rows = [
        jnp.concatenate([polar_ref[c * groups + k] for k in range(groups)], axis=1) for c in range(columns)
    ]
    product = lax.dot_general(
        jnp.concatenate(rows, axis=0),
        coulomb_ref[...].reshape(order, order),
        (((1,), (1,)), ((), ())),
        preferred_element_type=jnp.float32,
    )
    for c in range(columns):
        for part in range(2):
            at = (c * 2 + part) * here
            for k in range(groups):
                out_ref[pl.ds((c * groups + k) * 2 + part, here, stride=stride), :] = product[
                    at:at + here, k * LANES:(k + 1) * LANES
                ]


def tables(energies):
    points = energies * 2 // RADIX
    angle = np.outer(np.arange(points), np.arange(points)) % points * (2 * np.pi / points)
    cos, sin = np.cos(angle), np.sin(angle)
    whole = np.block([[cos, sin], [-sin, cos]])
    high = whole.astype(jnp.bfloat16)
    low = (whole - high.astype(np.float64)).astype(jnp.bfloat16)
    twiddle = np.zeros((points, LANES), np.float32)
    for r in range(RADIX):
        turned = np.arange(points) * r * (np.pi / energies)
        twiddle[:, 2 * r], twiddle[:, 2 * r + 1] = np.cos(turned), -np.sin(turned)
    return np.concatenate([high, low]), twiddle


def rows_view(x):
    energies, _, columns, order = x.shape
    x = x.reshape(energies, 2, columns, order // LANES, LANES).transpose(0, 2, 3, 1, 4)
    x = with_layout_constraint(x, Layout(tuple(range(x.ndim))))
    return x.reshape(-1, LANES)


def pack(lesser, greater, coulomb, owners):
    here = lesser.shape[0]
    lesser, greater = rows_view(lesser), rows_view(greater)
    return pl.pallas_call(
        pack_kernel,
        out_shape=jax.ShapeDtypeStruct((owners, 5 * here, LANES), jnp.float32),
        in_specs=[pl.BlockSpec(memory_space=pltpu.HBM)] * 3,
        out_specs=pl.BlockSpec(memory_space=pltpu.VMEM),
        scratch_shapes=[pltpu.VMEM(x.shape, x.dtype) for x in (lesser, greater, coulomb)]
        + [pltpu.SemaphoreType.DMA((3,))],
        compiler_params=pltpu.CompilerParams(vmem_limit_bytes=16 << 20),
        name="pack",
    )(*(pltpu.with_memory_space_constraint(x, pltpu.HBM) for x in (lesser, greater, coulomb)))


def unpack(x, wide, order):
    return pl.pallas_call(
        unpack_kernel,
        out_shape=jax.ShapeDtypeStruct((wide, order), jnp.bfloat16),
        compiler_params=pltpu.CompilerParams(vmem_limit_bytes=16 << 20),
        name="unpack",
    )(x)


def correlate(x):
    owners, here, lanes = x.shape[0], x.shape[1] // 5, x.shape[2]
    energies = owners * here
    points = energies * 2 // RADIX
    matrices, twiddle = tables(energies)
    return pl.pallas_call(
        correlate_kernel,
        out_shape=jax.ShapeDtypeStruct((owners, 2 * here, lanes), jnp.bfloat16),
        scratch_shapes=[
            pltpu.VMEM((4, 2, points, lanes), jnp.float32),
            pltpu.VMEM((2 * RADIX, points, lanes), jnp.float32),
        ],
        compiler_params=pltpu.CompilerParams(vmem_limit_bytes=24 << 20),
        cost_estimate=pl.CostEstimate(
            flops=RADIX * 3 * 2 * (2 * points) ** 2 * 3 * lanes, bytes_accessed=x.size * 4 + x.size, transcendentals=0
        ),
        name="correlate",
    )(x, jnp.asarray(matrices), jnp.asarray(twiddle))


def screen(polar, runs, place, shape):
    energies, _, columns, order = shape
    run, wide, _ = runs[0].shape
    out = pl.pallas_call(
        screen_kernel,
        out_shape=jax.ShapeDtypeStruct((energies * columns * order * 2 // LANES, LANES), jnp.float32),
        in_specs=[pl.BlockSpec(memory_space=pltpu.SMEM)]
        + [pl.BlockSpec(memory_space=pltpu.VMEM)] * (1 + len(runs)),
        out_specs=pl.BlockSpec(memory_space=pltpu.VMEM),
        scratch_shapes=[pltpu.VMEM((len(runs) * run, wide, order), jnp.bfloat16)],
        compiler_params=pltpu.CompilerParams(vmem_limit_bytes=24 << 20),
        name="screen",
    )(place, polar, *runs)
    out = out.reshape(energies, columns, order // LANES, 2, LANES).transpose(0, 1, 3, 2, 4)
    return out.reshape(energies, columns, 2, order).transpose(0, 2, 1, 3)


def moved(x, sharers, hops):
    def source(at):
        z, x, core = at // (ACROSS * CORES), at // CORES % ACROSS, at % CORES
        z, x, core = (z + hops[0]) % RUN, (x + hops[1]) % ACROSS, (core + hops[2]) % CORES
        return (z * ACROSS + x) * CORES + core

    return lax.ppermute(x, "col", [(source(at), at) for at in range(sharers)])


def per_device(lesser, greater_transposed, coulomb):
    owners = lax.axis_size("energy")
    sharers = lax.axis_size("col")
    order = lesser.shape[3]
    packed = pack(lesser, greater_transposed, coulomb, owners)
    got = lax.all_to_all(packed.astype(jnp.float16), "energy", split_axis=0, concat_axis=0, tiled=True)
    got = got.astype(jnp.float32)
    wide = coulomb.shape[1]
    mine = unpack(got, wide, order)
    run = jnp.stack([mine] + [moved(mine, sharers, (hop, 0, 0)) for hop in range(1, RUN)])
    polar = correlate(got)
    run, polar = lax.optimization_barrier((run, polar))
    ahead, behind = moved(run, sharers, (0, 1, 0)), moved(run, sharers, (0, ACROSS - 1, 0))
    runs = [run, ahead, behind, moved(behind, sharers, (0, ACROSS - 1, 0))]
    runs += [moved(run, sharers, (0, 0, 1)) for run in runs]
    polar = lax.all_to_all(polar, "energy", split_axis=0, concat_axis=0, tiled=True)
    at = lax.axis_index("col")
    place = [lax.div(at, ACROSS * CORES), lax.rem(lax.div(at, CORES), ACROSS), lax.rem(at, CORES)]
    return screen(polar, runs, jnp.stack(place).astype(jnp.int32), lesser.shape)


def solution(mesh):
    placed = (P("energy", None, "col", None), P("energy", None, "col", None), P("energy", "col"))
    return jax.shard_map(
        per_device,
        mesh=mesh,
        in_specs=placed,
        out_specs=P("energy", None, "col", None),
        check_vma=False,
    )
```
